32 devices in a mesh: grp: 2 (over y), seq: 4 (over z), ch: 2 (over x), sub: 2 (over core).
Axes of the slice: x: 2, y: 2, z: 4, core: 2. Of those that a mesh axis runs over, the one named last changes fastest.
Arguments:
- token_ids: int32 [2048], P(('grp', 'seq')), parts along dimension 0, may hold values from 0 to 511
- residual_in: bfloat16 [2048, 4096], P(('grp', 'seq'), ('ch', 'sub')), parts along dimension 0, may hold values from -6 to 6
- embedding: bfloat16 [512, 4096], P(None, ('ch', 'sub')), may hold values from -6 to 6
- in_weight: bfloat16 [4096, 3, 2048], P('seq', None, ('ch', 'sub')), may hold values from -0.09375 to 0.09375
- short_filter: float32 [3, 3, 2048], P(None, None, ('ch', 'sub')), may hold values from -3 to 3
- decay_rate: float32 [16, 2048], P(None, ('ch', 'sub')), may hold values from 1e-05 to 0.05
- residue: float32 [16, 2048], P(None, ('ch', 'sub')), may hold values from -0.24 to 0.24
- skip: float32 [2048], P(('ch', 'sub')), may hold values from -4 to 4
Outputs:
- mixed_out: bfloat16 [2048, 2048], P(('grp', 'seq'), ('ch', 'sub')), parts along dimension 0
The draws below stay inside these ranges and needn't reach their ends.
There are 2 independent parts, one for each index of `grp`. The reference program is written for one: setup_inputs(seed, part) draws one part's arguments, and reference() takes and returns one part's arrays. A program takes and returns all parts, laid end to end along the dimension named above; an argument that names none is the same for every part. Nothing has to cross between parts.
All inputs are finite; a program needn't handle non-finite values.
Results may differ from the reference program's by a relative error of at most 0.0095.
Values may be sent and summed in bfloat16 or wider, within the bound.
A program may use at most 64 MiB of HBM per device.

```python
import math
import jax
import jax.numpy as jnp
import numpy as np
from jax import lax

D = 4096
V = 512
C = 2048
MODES = 16
SHORT = 3
TOKENS = 1024


def modal_rates(key):
    sample = jax.random.uniform(jax.random.fold_in(key, 17), (MODES, C), jnp.float32)
    lower_end = 0.0001
    upper_end = 0.05
    return jnp.exp(jnp.log(lower_end) + sample * (jnp.log(upper_end) - jnp.log(lower_end)))


def draw_decay_rate(key, part):
    return modal_rates(key)


def draw_residue(key, part):
    rates = modal_rates(key)
    normal_part = jax.random.truncated_normal(jax.random.fold_in(key, 29), -3.0, 3.0, (MODES, C), jnp.float32)
    return normal_part * jnp.sqrt(2.0 * rates / 16.0)


def plant(drawn, rng, least, high):
    index_at = [jax.random.randint(jax.random.fold_in(rng, axis), (), 0, length) for axis, length in enumerate(drawn.shape)]
    main_axis = drawn.shape.index(max(drawn.shape))
    neighbour = index_at[:main_axis] + [(index_at[main_axis] + 1) % drawn.shape[main_axis]] + index_at[main_axis + 1:]
    return drawn.at[tuple(index_at)].set(least).at[tuple(neighbour)].set(high)


def level_of(own_key, extent, shards, least, high):
    factor_of, own = 1.0, jax.random.fold_in(own_key, 6)
    for dim, shards_of in shards:
        draws = jnp.exp(jax.random.uniform(jax.random.fold_in(own, dim), (shards_of,), jnp.float32, least / len(shards), high / len(shards)))
        factor_of = factor_of * jnp.repeat(draws, extent[dim] // shards_of).reshape([-1 if axis == dim else 1 for axis in range(len(extent))])
    return factor_of


def rank_table(number_of, lean):
    weights = [(1 << 20) // math.isqrt(standing ** lean) + 1 for standing in range(1, number_of + 1)]
    spread = 1 + sum(weights) // (1 << 30)
    return np.cumsum(np.array([max(1, weight // spread) for weight in weights]))


def skewed_ids(rng, dims, amount, skew):
    grid = rank_table(amount, skew)
    pick = jax.random.randint(jax.random.fold_in(rng, 1), dims, 0, int(grid[amount - 1]))
    standing = jnp.searchsorted(jnp.asarray(grid, jnp.int32), pick, side="right")
    return jax.random.permutation(jax.random.fold_in(rng, 2), amount)[standing].astype(jnp.int32)


def noise(rng, extent, deviation, most, pieces=(), held_as=jnp.bfloat16):
    result = deviation * jax.random.normal(rng, extent, jnp.float32)
    if pieces:
        result = result * level_of(rng, extent, pieces, -0.22, 0.18)
    return jnp.clip(result, -most, most).astype(held_as)


def setup_inputs(seed: int = 0, part: int = 0) -> dict:
    key_of = jax.random.split(jax.random.key(seed), 9)
    own_keys = jax.random.split(jax.random.fold_in(key_of[8], part), 9)
    token_ids = plant(skewed_ids(own_keys[0], (TOKENS,), V, 2), jax.random.fold_in(own_keys[0], 3), 0, V - 1).astype(jnp.int32)
    residual_in = noise(own_keys[1], (TOKENS, D), 1.0, 6.0, ((0, 4), (1, 4)))
    embedding = noise(key_of[2], (V, D), 1.0, 6.0, ((1, 4),))
    in_weight = noise(key_of[3], (D, 3, C), D ** -0.5, 0.09375, ((0, 4), (2, 4)))
    short_filter = noise(key_of[4], (SHORT, 3, C), 0.5, 3.0, ((2, 4),), jnp.float32)
    decay_rate = draw_decay_rate(jax.random.fold_in(key_of[8], 71), part)
    residue = draw_residue(jax.random.fold_in(key_of[8], 71), part)
    skip = noise(key_of[7], (C,), 1.0, 4.0, ((0, 4),), jnp.float32)
    return {"token_ids": token_ids, "residual_in": residual_in, "embedding": embedding, "in_weight": in_weight, "short_filter": short_filter, "decay_rate": decay_rate, "residue": residue, "skip": skip}


def reference(token_ids, residual_in, embedding, in_weight, short_filter, decay_rate, residue, skip):
    embedded = jnp.take(embedding, token_ids, axis=0).astype(jnp.float32)
    inputs = (residual_in.astype(jnp.float32) + embedded).astype(jnp.bfloat16)
    projected = jnp.dot(inputs, in_weight.reshape(D, 3 * C), preferred_element_type=jnp.float32)
    projected = lax.optimization_barrier(projected.astype(jnp.bfloat16)).reshape(TOKENS, 3, C).astype(jnp.float32)
    zero_rows = jnp.zeros((2, 3, C), jnp.float32)
    padded = jnp.concatenate([zero_rows, projected], axis=0)
    mixed_in = short_filter[0] * padded[2:] + short_filter[1] * padded[1:-1] + short_filter[2] * padded[:-2]
    query_gate = mixed_in[:, 0]
    product = lax.optimization_barrier((mixed_in[:, 1] * mixed_in[:, 2]).astype(jnp.bfloat16)).astype(jnp.float32)
    delay_steps = jnp.arange(TOKENS).astype(jnp.float32)[:, None]
    filter_taps = jnp.zeros((TOKENS, C), jnp.float32)
    for mode_index in range(MODES):
        filter_taps = filter_taps + residue[mode_index] * jnp.exp(-decay_rate[mode_index] * delay_steps)
    spec_input = jnp.fft.rfft(product, n=2 * TOKENS, axis=0)
    spec_filter = jnp.fft.rfft(filter_taps, n=2 * TOKENS, axis=0)
    conv_out = jnp.fft.irfft(spec_input * spec_filter, n=2 * TOKENS, axis=0)[:TOKENS].astype(jnp.float32)
    return (query_gate * (conv_out + skip * product)).astype(jnp.bfloat16)
```

```python
import functools

import jax
import jax.numpy as jnp
from jax import lax
from jax.experimental import pallas as pl
from jax.experimental.pallas import tpu as pltpu
from jax.sharding import PartitionSpec as P

PRECISE = lax.Precision.HIGHEST
TWO_PI = 6.283185307179586


def shifted(x, axis, by):
    peers = lax.axis_size(axis)
    pairs = [(i, i + by) for i in range(peers) if 0 <= i + by < peers]
    return lax.ppermute(x, axis, pairs)


def swapped(value, axis, apart):
    mask = 2**apart
    pairs = [(source, source ^ mask) for source in range(lax.axis_size(axis))]
    return lax.ppermute(value, axis, pairs)


def reversed_bits(number, bit_count):
    result = jnp.zeros_like(number)
    for section_bit in range(bit_count):
        result = result + (number >> section_bit & 1) * (1 << bit_count - 1 - section_bit)
    return result


def angle_table(left_idx, right_idx, period):
    wrapped = left_idx[:, None] * right_idx[None, :] % period
    return TWO_PI * wrapped.astype(jnp.float32) / period


def complex_mix(mat_re, mat_im, data_re, data_im):
    real_part = jnp.einsum("kr,rjc->kjc", mat_re, data_re, precision=PRECISE) - jnp.einsum(
        "kr,rjc->kjc", mat_im, data_im, precision=PRECISE
    )
    imag_part = jnp.einsum("kr,rjc->kjc", mat_re, data_im, precision=PRECISE) + jnp.einsum(
        "kr,rjc->kjc", mat_im, data_re, precision=PRECISE
    )
    return (real_part, imag_part)


def complex_dot(mat_re, mat_im, data_re, data_im):
    real_part = jnp.dot(mat_re, data_re, precision=PRECISE) - jnp.dot(
        mat_im, data_im, precision=PRECISE
    )
    imag_part = jnp.dot(mat_re, data_im, precision=PRECISE) + jnp.dot(
        mat_im, data_re, precision=PRECISE
    )
    return (real_part, imag_part)


def shards(token_ids, residual_in, embedding, in_weight, short_filter, decay_rate, residue, skip):
    tok_rows = residual_in.shape[0]
    vocab_size = embedding.shape[0]
    channels = skip.shape[0]
    seq_parts = lax.axis_size("seq")
    bit_count = seq_parts.bit_length() - 1
    my_index = lax.axis_index("seq")
    length = tok_rows * seq_parts
    padded_len = 2 * length
    group_rows = tok_rows // seq_parts
    onehot = (token_ids[:, None] == jnp.arange(vocab_size, dtype=jnp.int32)[None, :]).astype(
        jnp.bfloat16
    )
    embedded = jnp.dot(onehot, embedding, preferred_element_type=jnp.float32)
    inputs = (residual_in.astype(jnp.float32) + embedded).astype(jnp.bfloat16)
    features = lax.all_gather(inputs, ("ch", "sub"), axis=1, tiled=True)
    piece_rows = lax.all_gather(in_weight, "seq", axis=0, tiled=True)
    flat_piece = piece_rows.reshape(piece_rows.shape[0], 3 * channels)
    projected = jnp.dot(features, flat_piece, preferred_element_type=jnp.float32)
    projected = projected.astype(jnp.bfloat16).reshape(tok_rows, 3, channels)
    rim_rows = shifted(projected[tok_rows - 2 :], "seq", 1)
    extended = jnp.concatenate([rim_rows, projected], axis=0).astype(jnp.float32)
    mixed_in = (
        short_filter[0] * extended[2:]
        + short_filter[1] * extended[1:-1]
        + short_filter[2] * extended[:-2]
    )
    query_gate = mixed_in[:, 0]
    product = (mixed_in[:, 1] * mixed_in[:, 2]).astype(jnp.bfloat16)
    local_pos = jnp.arange(tok_rows, dtype=jnp.int32)
    sources = jnp.arange(seq_parts, dtype=jnp.int32)
    within_rows = my_index * group_rows + jnp.arange(group_rows, dtype=jnp.int32)
    block_pos = sources[:, None] * tok_rows + within_rows[None, :]
    block_angle = TWO_PI * block_pos.astype(jnp.float32) / padded_len
    pos_angle = TWO_PI * (my_index * tok_rows + local_pos).astype(jnp.float32) / padded_len
    values = product.astype(jnp.float32)
    state_re = jnp.concatenate([values, values * jnp.cos(pos_angle)[:, None]], -1)
    state_im = jnp.concatenate([jnp.zeros_like(values), -values * jnp.sin(pos_angle)[:, None]], -1)
    state_now = jnp.stack([state_re, state_im])
    for section_bit in range(bit_count - 1, -1, -1):
        half_span = 1 << section_bit
        partner = swapped(state_now.astype(jnp.bfloat16), "seq", section_bit).astype(
            state_now.dtype
        )
        upper_half = my_index >> section_bit & 1 == 1
        phase_now = TWO_PI * (my_index % half_span).astype(jnp.float32) / (2 * half_span)
        difference = partner - state_now
        rot_re = difference[0] * jnp.cos(phase_now) + difference[1] * jnp.sin(phase_now)
        rot_im = difference[1] * jnp.cos(phase_now) - difference[0] * jnp.sin(phase_now)
        state_now = jnp.where(upper_half, jnp.stack([rot_re, rot_im]), state_now + partner)
    own_freq = reversed_bits(my_index, bit_count)
    holders = reversed_bits(sources, bit_count)
    twist_angle = TWO_PI * (local_pos * own_freq % length).astype(jnp.float32) / length
    twist_re = jnp.cos(twist_angle)[:, None]
    twist_im = -jnp.sin(twist_angle)[:, None]
    spec_re = state_now[0] * twist_re - state_now[1] * twist_im
    spec_im = state_now[0] * twist_im + state_now[1] * twist_re
    kernel_table = angle_table(local_pos, local_pos, tok_rows)
    dft_re = jnp.cos(kernel_table)
    dft_im = -jnp.sin(kernel_table)
    spec_re, spec_im = complex_dot(dft_re, dft_im, spec_re, spec_im)
    parity = (jnp.arange(2 * channels, dtype=jnp.int32) >= channels).astype(jnp.int32)
    full_freq = 2 * (own_freq + seq_parts * local_pos)[:, None] + parity[None, :]
    freq_angle = TWO_PI * full_freq.astype(jnp.float32) / padded_len
    half_sine = jnp.sin(0.5 * freq_angle)
    sine_full = jnp.sin(freq_angle)
    sign_flip = 1.0 - 2.0 * parity.astype(jnp.float32)
    rates_both = jnp.concatenate([decay_rate, decay_rate], -1)
    residues_both = jnp.concatenate([residue, residue], -1)
    filt_re = jnp.zeros_like(spec_re)
    filt_im = jnp.zeros_like(spec_re)
    for mode_index in range(rates_both.shape[0]):
        rate_now = rates_both[mode_index]
        decay_now = jnp.exp(-rate_now)
        numerator = residues_both[mode_index] * (1.0 - sign_flip * jnp.exp(-rate_now * length))
        denom_re = -jnp.expm1(-rate_now) + 2.0 * decay_now * half_sine * half_sine
        denom_im = decay_now * sine_full
        scaled = numerator / (denom_re * denom_re + denom_im * denom_im)
        filt_re = filt_re + scaled * denom_re
        filt_im = filt_im - scaled * denom_im
    prod_re = spec_re * filt_re - spec_im * filt_im
    prod_im = spec_re * filt_im + spec_im * filt_re
    inv_re, inv_im = complex_dot(dft_re, -dft_im, prod_re, prod_im)
    back_re = inv_re * twist_re + inv_im * twist_im
    back_im = inv_im * twist_re - inv_re * twist_im
    returned = lax.all_to_all(
        jnp.stack([back_re, back_im]).reshape(2, 1, tok_rows, 2 * channels).astype(jnp.bfloat16),
        "seq",
        split_axis=2,
        concat_axis=1,
        tiled=True,
    ).astype(jnp.float32)
    inverse_angle = angle_table(sources, holders, seq_parts)
    block_re, block_im = complex_mix(
        jnp.cos(inverse_angle), jnp.sin(inverse_angle), returned[0], returned[1]
    )
    conv_blocks = (
        block_re[..., :channels]
        + jnp.cos(block_angle)[:, :, None] * block_re[..., channels:]
        - jnp.sin(block_angle)[:, :, None] * block_im[..., channels:]
    )
    conv_blocks = conv_blocks / padded_len
    conv_rows = lax.all_to_all(conv_blocks, "seq", split_axis=0, concat_axis=1, tiled=True)[0]
    mixed_out = (query_gate * (conv_rows + skip * product.astype(jnp.float32))).astype(jnp.bfloat16)
    return mixed_out


def mix_and_scan(rows, modes, part_ref, taps_ref, rate_ref, residue_ref, skip_ref, out_ref, proj, values, gate, result):
    total, lanes = out_ref.shape
    lead = proj.shape[1] - total
    taps_count = taps_ref.shape[0]
    span = total // rows
    for g in range(3):
        proj[g, :lead, :] = jnp.zeros((lead, lanes), jnp.float32)
    parts = part_ref.shape[0]

    @pl.loop(0, 3)
    def _(g):
        acc = part_ref[0, g].astype(jnp.float32)
        for i in range(1, parts):
            acc = acc + part_ref[i, g].astype(jnp.float32)
        proj[g, lead:, :] = acc.astype(jnp.bfloat16).astype(jnp.float32)

    mixed = []
    for g in range(3):
        acc = None
        for i in range(taps_count):
            term = taps_ref[i, g : g + 1, :] * proj[g, pl.ds(lead - i, total), :]
            acc = term if acc is None else acc + term
        if g == 0:
            gate[...] = acc
        else:
            mixed.append(acc)
    values[...] = (mixed[0] * mixed[1]).astype(jnp.bfloat16).astype(jnp.float32)

    decay = [jnp.broadcast_to(jnp.exp(-rate_ref[m : m + 1, :]), (rows, lanes)) for m in range(modes)]
    zero = jnp.zeros((rows, lanes), jnp.float32)

    def ends(j, state):
        now = values[pl.ds(j, rows, stride=span), :]
        return tuple(u * d + now for u, d in zip(state, decay))

    state = lax.fori_loop(0, span, ends, (zero,) * modes, unroll=4)
    index = lax.broadcasted_iota(jnp.int32, (rows, lanes), 0)

    def down(x, by):
        return jnp.where(index >= by, pltpu.roll(x, by, 0), 0.0)

    entering = []
    for m in range(modes):
        carry = down(state[m], 1)
        by = 1
        while by < rows:
            carry = carry + jnp.exp(-rate_ref[m : m + 1, :] * (span * by)) * down(carry, by)
            by *= 2
        entering.append(carry)
    weight = [jnp.broadcast_to(residue_ref[m : m + 1, :], (rows, lanes)) for m in range(modes)]
    direct = jnp.broadcast_to(skip_ref[...], (rows, lanes))

    def scan(j, state):
        at = pl.ds(j, rows, stride=span)
        now = values[at, :]
        state = tuple(u * d + now for u, d in zip(state, decay))
        terms = [u * w for u, w in zip(state, weight)] + [direct * now]
        while len(terms) > 1:
            terms = [a + b for a, b in zip(terms[::2], terms[1::2])] + terms[len(terms) // 2 * 2 :]
        result[at, :] = gate[at, :] * terms[0]
        return state

    lax.fori_loop(0, span, scan, tuple(entering), unroll=4)
    out_ref[...] = result[...].astype(out_ref.dtype)


def convolved(partial, short_filter, decay_rate, residue, skip):
    parts, _, total, lanes = partial.shape
    modes = decay_rate.shape[0]
    rows = 8
    f32 = jnp.float32
    return pl.pallas_call(
        functools.partial(mix_and_scan, rows, modes),
        out_shape=jax.ShapeDtypeStruct((total, lanes), jnp.bfloat16),
        in_specs=[pl.BlockSpec(memory_space=pltpu.VMEM)] * 5,
        out_specs=pl.BlockSpec(memory_space=pltpu.VMEM),
        scratch_shapes=[
            pltpu.VMEM((3, total + 8, lanes), f32),
            pltpu.VMEM((total, lanes), f32),
            pltpu.VMEM((total, lanes), f32),
            pltpu.VMEM((total, lanes), f32),
        ],
        compiler_params=pltpu.CompilerParams(vmem_limit_bytes=40 * 2**20),
    )(partial, short_filter, decay_rate, residue, skip.reshape(1, lanes))


def fast_shards(token_ids, residual_in, embedding, in_weight, short_filter, decay_rate, residue, skip):
    tok_rows, width = residual_in.shape
    vocab_size = embedding.shape[0]
    channels = skip.shape[0]
    seq_parts = lax.axis_size("seq")
    me = lax.axis_index("seq")
    lanes = channels // seq_parts
    total = tok_rows * seq_parts
    onehot = (token_ids[:, None] == jnp.arange(vocab_size, dtype=jnp.int32)[None, :]).astype(jnp.bfloat16)
    embedded = jnp.dot(onehot, embedding, preferred_element_type=jnp.float32)
    inputs = (residual_in.astype(jnp.float32) + embedded).astype(jnp.bfloat16)
    pairs = [(i * seq_parts + j, j * seq_parts + i) for i in range(seq_parts) for j in range(seq_parts)]
    turned = lax.ppermute(inputs, ("seq", "ch", "sub"), pairs)
    rows_all = lax.all_gather(turned, ("ch", "sub"), axis=0, tiled=True)
    weight = in_weight.transpose(1, 0, 2).reshape(3, width, seq_parts, lanes)
    partial = jnp.einsum("td,gdsc->sgtc", rows_all, weight, preferred_element_type=jnp.float32).astype(jnp.bfloat16)
    partial = lax.all_to_all(partial, "seq", split_axis=0, concat_axis=0, tiled=True)

    def own(x):
        return lax.dynamic_slice_in_dim(x, me * lanes, lanes, axis=x.ndim - 1)

    mixed = convolved(partial, own(short_filter), own(decay_rate), own(residue), own(skip))
    return lax.all_to_all(mixed, "seq", split_axis=0, concat_axis=1, tiled=True)


def fits(mesh):
    seq_parts = mesh.shape["seq"]
    return seq_parts == mesh.shape["ch"] * mesh.shape["sub"]


def solution(mesh):
    return jax.shard_map(
        fast_shards if fits(mesh) else shards,
        mesh=mesh,
        in_specs=(
            P(("grp", "seq")),
            P(("grp", "seq"), ("ch", "sub")),
            P(None, ("ch", "sub")),
            P("seq", None, ("ch", "sub")),
            P(None, None, ("ch", "sub")),
            P(None, ("ch", "sub")),
            P(None, ("ch", "sub")),
            P(("ch", "sub")),
        ),
        out_specs=P(("grp", "seq"), ("ch", "sub")),
        check_vma=False,
    )
```

```python
import functools

import jax
import jax.numpy as jnp
from jax import lax
from jax.experimental import pallas as pl
from jax.experimental.pallas import tpu as pltpu
from jax.sharding import PartitionSpec as P

PRECISE = lax.Precision.HIGHEST
TWO_PI = 6.283185307179586


def shifted(x, axis, by):
    peers = lax.axis_size(axis)
    pairs = [(i, i + by) for i in range(peers) if 0 <= i + by < peers]
    return lax.ppermute(x, axis, pairs)


def swapped(value, axis, apart):
    mask = 2**apart
    pairs = [(source, source ^ mask) for source in range(lax.axis_size(axis))]
    return lax.ppermute(value, axis, pairs)


def reversed_bits(number, bit_count):
    result = jnp.zeros_like(number)
    for section_bit in range(bit_count):
        result = result + (number >> section_bit & 1) * (1 << bit_count - 1 - section_bit)
    return result


def angle_table(left_idx, right_idx, period):
    wrapped = left_idx[:, None] * right_idx[None, :] % period
    return TWO_PI * wrapped.astype(jnp.float32) / period


def complex_mix(mat_re, mat_im, data_re, data_im):
    real_part = jnp.einsum("kr,rjc->kjc", mat_re, data_re, precision=PRECISE) - jnp.einsum(
        "kr,rjc->kjc", mat_im, data_im, precision=PRECISE
    )
    imag_part = jnp.einsum("kr,rjc->kjc", mat_re, data_im, precision=PRECISE) + jnp.einsum(
        "kr,rjc->kjc", mat_im, data_re, precision=PRECISE
    )
    return (real_part, imag_part)


def complex_dot(mat_re, mat_im, data_re, data_im):
    real_part = jnp.dot(mat_re, data_re, precision=PRECISE) - jnp.dot(
        mat_im, data_im, precision=PRECISE
    )
    imag_part = jnp.dot(mat_re, data_im, precision=PRECISE) + jnp.dot(
        mat_im, data_re, precision=PRECISE
    )
    return (real_part, imag_part)


def shards(token_ids, residual_in, embedding, in_weight, short_filter, decay_rate, residue, skip):
    tok_rows = residual_in.shape[0]
    vocab_size = embedding.shape[0]
    channels = skip.shape[0]
    seq_parts = lax.axis_size("seq")
    bit_count = seq_parts.bit_length() - 1
    my_index = lax.axis_index("seq")
    length = tok_rows * seq_parts
    padded_len = 2 * length
    group_rows = tok_rows // seq_parts
    onehot = (token_ids[:, None] == jnp.arange(vocab_size, dtype=jnp.int32)[None, :]).astype(
        jnp.bfloat16
    )
    embedded = jnp.dot(onehot, embedding, preferred_element_type=jnp.float32)
    inputs = (residual_in.astype(jnp.float32) + embedded).astype(jnp.bfloat16)
    features = lax.all_gather(inputs, ("ch", "sub"), axis=1, tiled=True)
    piece_rows = lax.all_gather(in_weight, "seq", axis=0, tiled=True)
    flat_piece = piece_rows.reshape(piece_rows.shape[0], 3 * channels)
    projected = jnp.dot(features, flat_piece, preferred_element_type=jnp.float32)
    projected = projected.astype(jnp.bfloat16).reshape(tok_rows, 3, channels)
    rim_rows = shifted(projected[tok_rows - 2 :], "seq", 1)
    extended = jnp.concatenate([rim_rows, projected], axis=0).astype(jnp.float32)
    mixed_in = (
        short_filter[0] * extended[2:]
        + short_filter[1] * extended[1:-1]
        + short_filter[2] * extended[:-2]
    )
    query_gate = mixed_in[:, 0]
    product = (mixed_in[:, 1] * mixed_in[:, 2]).astype(jnp.bfloat16)
    local_pos = jnp.arange(tok_rows, dtype=jnp.int32)
    sources = jnp.arange(seq_parts, dtype=jnp.int32)
    within_rows = my_index * group_rows + jnp.arange(group_rows, dtype=jnp.int32)
    block_pos = sources[:, None] * tok_rows + within_rows[None, :]
    block_angle = TWO_PI * block_pos.astype(jnp.float32) / padded_len
    pos_angle = TWO_PI * (my_index * tok_rows + local_pos).astype(jnp.float32) / padded_len
    values = product.astype(jnp.float32)
    state_re = jnp.concatenate([values, values * jnp.cos(pos_angle)[:, None]], -1)
    state_im = jnp.concatenate([jnp.zeros_like(values), -values * jnp.sin(pos_angle)[:, None]], -1)
    state_now = jnp.stack([state_re, state_im])
    for section_bit in range(bit_count - 1, -1, -1):
        half_span = 1 << section_bit
        partner = swapped(state_now.astype(jnp.bfloat16), "seq", section_bit).astype(
            state_now.dtype
        )
        upper_half = my_index >> section_bit & 1 == 1
        phase_now = TWO_PI * (my_index % half_span).astype(jnp.float32) / (2 * half_span)
        difference = partner - state_now
        rot_re = difference[0] * jnp.cos(phase_now) + difference[1] * jnp.sin(phase_now)
        rot_im = difference[1] * jnp.cos(phase_now) - difference[0] * jnp.sin(phase_now)
        state_now = jnp.where(upper_half, jnp.stack([rot_re, rot_im]), state_now + partner)
    own_freq = reversed_bits(my_index, bit_count)
    holders = reversed_bits(sources, bit_count)
    twist_angle = TWO_PI * (local_pos * own_freq % length).astype(jnp.float32) / length
    twist_re = jnp.cos(twist_angle)[:, None]
    twist_im = -jnp.sin(twist_angle)[:, None]
    spec_re = state_now[0] * twist_re - state_now[1] * twist_im
    spec_im = state_now[0] * twist_im + state_now[1] * twist_re
    kernel_table = angle_table(local_pos, local_pos, tok_rows)
    dft_re = jnp.cos(kernel_table)
    dft_im = -jnp.sin(kernel_table)
    spec_re, spec_im = complex_dot(dft_re, dft_im, spec_re, spec_im)
    parity = (jnp.arange(2 * channels, dtype=jnp.int32) >= channels).astype(jnp.int32)
    full_freq = 2 * (own_freq + seq_parts * local_pos)[:, None] + parity[None, :]
    freq_angle = TWO_PI * full_freq.astype(jnp.float32) / padded_len
    half_sine = jnp.sin(0.5 * freq_angle)
    sine_full = jnp.sin(freq_angle)
    sign_flip = 1.0 - 2.0 * parity.astype(jnp.float32)
    rates_both = jnp.concatenate([decay_rate, decay_rate], -1)
    residues_both = jnp.concatenate([residue, residue], -1)
    filt_re = jnp.zeros_like(spec_re)
    filt_im = jnp.zeros_like(spec_re)
    for mode_index in range(rates_both.shape[0]):
        rate_now = rates_both[mode_index]
        decay_now = jnp.exp(-rate_now)
        numerator = residues_both[mode_index] * (1.0 - sign_flip * jnp.exp(-rate_now * length))
        denom_re = -jnp.expm1(-rate_now) + 2.0 * decay_now * half_sine * half_sine
        denom_im = decay_now * sine_full
        scaled = numerator / (denom_re * denom_re + denom_im * denom_im)
        filt_re = filt_re + scaled * denom_re
        filt_im = filt_im - scaled * denom_im
    prod_re = spec_re * filt_re - spec_im * filt_im
    prod_im = spec_re * filt_im + spec_im * filt_re
    inv_re, inv_im = complex_dot(dft_re, -dft_im, prod_re, prod_im)
    back_re = inv_re * twist_re + inv_im * twist_im
    back_im = inv_im * twist_re - inv_re * twist_im
    returned = lax.all_to_all(
        jnp.stack([back_re, back_im]).reshape(2, 1, tok_rows, 2 * channels).astype(jnp.bfloat16),
        "seq",
        split_axis=2,
        concat_axis=1,
        tiled=True,
    ).astype(jnp.float32)
    inverse_angle = angle_table(sources, holders, seq_parts)
    block_re, block_im = complex_mix(
        jnp.cos(inverse_angle), jnp.sin(inverse_angle), returned[0], returned[1]
    )
    conv_blocks = (
        block_re[..., :channels]
        + jnp.cos(block_angle)[:, :, None] * block_re[..., channels:]
        - jnp.sin(block_angle)[:, :, None] * block_im[..., channels:]
    )
    conv_blocks = conv_blocks / padded_len
    conv_rows = lax.all_to_all(conv_blocks, "seq", split_axis=0, concat_axis=1, tiled=True)[0]
    mixed_out = (query_gate * (conv_rows + skip * product.astype(jnp.float32))).astype(jnp.bfloat16)
    return mixed_out


def mix_and_scan(rows, modes, part_ref, taps_ref, rate_ref, residue_ref, skip_ref, out_ref, proj, values, gate, result):
    total, lanes = out_ref.shape
    lead = proj.shape[1] - total
    taps_count = taps_ref.shape[0]
    span = total // rows
    for g in range(3):
        proj[g, :lead, :] = jnp.zeros((lead, lanes), jnp.float32)
    parts = part_ref.shape[0]

    @pl.loop(0, 3)
    def _(g):
        acc = part_ref[0, g].astype(jnp.float32)
        for i in range(1, parts):
            acc = acc + part_ref[i, g].astype(jnp.float32)
        proj[g, lead:, :] = acc.astype(jnp.bfloat16).astype(jnp.float32)

    mixed = []
    for g in range(3):
        acc = None
        for i in range(taps_count):
            term = taps_ref[i, g : g + 1, :] * proj[g, pl.ds(lead - i, total), :]
            acc = term if acc is None else acc + term
        if g == 0:
            gate[...] = acc
        else:
            mixed.append(acc)
    values[...] = (mixed[0] * mixed[1]).astype(jnp.bfloat16).astype(jnp.float32)

    decay = [jnp.broadcast_to(jnp.exp(-rate_ref[m : m + 1, :]), (rows, lanes)) for m in range(modes)]
    zero = jnp.zeros((rows, lanes), jnp.float32)

    def ends(j, state):
        now = values[pl.ds(j, rows, stride=span), :]
        return tuple(u * d + now for u, d in zip(state, decay))

    state = lax.fori_loop(0, span, ends, (zero,) * modes, unroll=4)
    index = lax.broadcasted_iota(jnp.int32, (rows, lanes), 0)

    def down(x, by):
        return jnp.where(index >= by, pltpu.roll(x, by, 0), 0.0)

    entering = []
    for m in range(modes):
        carry = down(state[m], 1)
        by = 1
        while by < rows:
            carry = carry + jnp.exp(-rate_ref[m : m + 1, :] * (span * by)) * down(carry, by)
            by *= 2
        entering.append(carry)
    weight = [jnp.broadcast_to(residue_ref[m : m + 1, :], (rows, lanes)) for m in range(modes)]
    direct = jnp.broadcast_to(skip_ref[...], (rows, lanes))

    def scan(j, state):
        at = pl.ds(j, rows, stride=span)
        now = values[at, :]
        state = tuple(u * d + now for u, d in zip(state, decay))
        terms = [u * w for u, w in zip(state, weight)] + [direct * now]
        while len(terms) > 1:
            terms = [a + b for a, b in zip(terms[::2], terms[1::2])] + terms[len(terms) // 2 * 2 :]
        result[at, :] = gate[at, :] * terms[0]
        return state

    lax.fori_loop(0, span, scan, tuple(entering), unroll=4)
    out_ref[...] = result[...].astype(out_ref.dtype)


def convolved(partial, short_filter, decay_rate, residue, skip):
    parts, _, total, lanes = partial.shape
    modes = decay_rate.shape[0]
    rows = 8
    f32 = jnp.float32
    return pl.pallas_call(
        functools.partial(mix_and_scan, rows, modes),
        out_shape=jax.ShapeDtypeStruct((total, lanes), jnp.bfloat16),
        in_specs=[pl.BlockSpec(memory_space=pltpu.VMEM)] * 5,
        out_specs=pl.BlockSpec(memory_space=pltpu.VMEM),
        scratch_shapes=[
            pltpu.VMEM((3, total + 8, lanes), f32),
            pltpu.VMEM((total, lanes), f32),
            pltpu.VMEM((total, lanes), f32),
            pltpu.VMEM((total, lanes), f32),
        ],
        compiler_params=pltpu.CompilerParams(vmem_limit_bytes=40 * 2**20),
    )(partial, short_filter, decay_rate, residue, skip.reshape(1, lanes))


MESH = pl.DeviceIdType.MESH


def partial_sums(parts, subs, x_ref, w_ref, out_ref, held, outbox, from_below, from_above, acc, x_send, x_recv, box_send, below_recv, above_recv):
    z = lax.axis_index("seq")
    ch = lax.axis_index("ch")
    sub = lax.axis_index("sub")
    k = ch * subs + sub
    rows = x_ref.shape[0]
    half = rows // 2
    lanes = w_ref.shape[2] // parts
    above = {"seq": lax.rem(z + 1, parts)}
    below = {"seq": lax.rem(z + parts - 1, parts)}
    turned = {"seq": k, "ch": z // subs, "sub": lax.rem(z, subs)}
    sibling = {"sub": 1 - sub}
    across = {"ch": 1 - ch}
    moves = k != z

    barrier = pltpu.get_barrier_semaphore()

    def greet(device):
        pl.semaphore_signal(barrier, inc=1, device_id=device, device_id_type=MESH)

    greet(sibling)
    greet(across)

    @pl.when(moves)
    def _():
        greet(turned)

    @pl.when(z > 0)
    def _():
        greet(below)

    @pl.when(z < parts - 1)
    def _():
        greet(above)

    peers = 2 + moves.astype(jnp.int32) + (z > 0).astype(jnp.int32) + (z < parts - 1).astype(jnp.int32)
    pl.semaphore_wait(barrier, peers)

    def piece(h):
        return pl.ds(h * half, half)

    def copy_x(kind, h, src, slot, device):
        return pltpu.make_async_remote_copy(
            src_ref=src,
            dst_ref=held.at[slot, piece(h)],
            send_sem=x_send.at[kind, h],
            recv_sem=x_recv.at[kind, h],
            device_id=device,
            device_id_type=MESH,
        )

    k_sibling = ch * subs + 1 - sub
    k_across = (1 - ch) * subs + sub
    k_far = (1 - ch) * subs + 1 - sub

    @pl.when(moves)
    def _():
        for h in range(2):
            copy_x(0, h, x_ref.at[piece(h)], z, turned).start()

    @pl.when(jnp.logical_not(moves))
    def _():
        for h in range(2):
            pltpu.make_async_copy(x_ref.at[piece(h)], held.at[k, piece(h)], x_recv.at[0, h]).start()

    for h in range(2):
        @pl.when(moves)
        def _():
            copy_x(0, h, x_ref.at[piece(h)], k, turned).wait_recv()

        @pl.when(jnp.logical_not(moves))
        def _():
            pltpu.make_async_copy(x_ref.at[piece(h)], held.at[k, piece(h)], x_recv.at[0, h]).wait()

        copy_x(1, h, held.at[k, piece(h)], k, across).start()
        copy_x(2, h, held.at[k, piece(h)], k, sibling).start()
    for h in range(2):
        copy_x(1, h, held.at[k, piece(h)], k_across, across).wait_recv()
        copy_x(3, h, held.at[k_across, piece(h)], k_across, sibling).start()
    for h in range(2):
        copy_x(2, h, held.at[k, piece(h)], k_sibling, sibling).wait_recv()
        copy_x(3, h, held.at[k_across, piece(h)], k_far, sibling).wait_recv()

    def own(j, h):
        at = pl.ds(pl.multiple_of(j * lanes, lanes), lanes)
        columns = jnp.concatenate([w_ref[g, :, at] for g in range(3)], axis=1)
        acc[...] = jnp.dot(held[h], columns, preferred_element_type=jnp.float32)

    def rising(j, h):
        return pltpu.make_async_remote_copy(
            src_ref=outbox.at[j, h],
            dst_ref=from_below.at[j, h],
            send_sem=box_send.at[j, h],
            recv_sem=below_recv.at[j, h],
            device_id=above,
            device_id_type=MESH,
        )

    def falling(j, h):
        return pltpu.make_async_remote_copy(
            src_ref=outbox.at[j, h],
            dst_ref=from_above.at[j, h],
            send_sem=box_send.at[j, h],
            recv_sem=above_recv.at[j, h],
            device_id=below,
            device_id_type=MESH,
        )

    def add_below(j, h):
        @pl.when(z > 0)
        def _():
            rising(j, h).wait_recv()
            acc[...] += from_below[j, h].astype(jnp.float32)

    def add_above(j, h):
        @pl.when(z < parts - 1)
        def _():
            falling(j, h).wait_recv()
            acc[...] += from_above[j, h].astype(jnp.float32)

    def step(u, _):
        i = u // parts
        h = lax.rem(u, parts)
        up = parts - 1 - i

        @pl.when(up > z)
        def _():
            own(up, h)
            add_below(up, h)
            outbox[up, h] = acc[...].astype(jnp.bfloat16)
            rising(up, h).start()

        @pl.when(i < z)
        def _():
            own(i, h)
            add_above(i, h)
            outbox[i, h] = acc[...].astype(jnp.bfloat16)
            falling(i, h).start()

        return 0

    lax.fori_loop(0, (parts - 1) * parts, step, 0)

    def last(h, _):
        own(z, h)
        add_below(z, h)
        add_above(z, h)
        for g in range(3):
            out_ref[0, g, pl.ds(pl.multiple_of(h * rows, rows), rows), :] = acc[:, g * lanes : (g + 1) * lanes].astype(jnp.bfloat16)
        return 0

    lax.fori_loop(0, parts, last, 0)

    def drain(u, _):
        j = u // parts
        h = lax.rem(u, parts)

        @pl.when(j != z)
        def _():
            rising(j, h).wait_send()

        return 0

    lax.fori_loop(0, parts * parts, drain, 0)

    @pl.when(moves)
    def _():
        for h in range(2):
            copy_x(0, h, x_ref.at[piece(h)], z, turned).wait_send()

    for h in range(2):
        copy_x(1, h, held.at[k, piece(h)], k, across).wait_send()
        copy_x(2, h, held.at[k, piece(h)], k, sibling).wait_send()
        copy_x(3, h, held.at[k_across, piece(h)], k_across, sibling).wait_send()


def summed(inputs, weight, parts, subs):
    rows, width = inputs.shape
    lanes = weight.shape[2] // parts
    box = (parts, parts, rows, 3 * lanes)
    dma = pltpu.SemaphoreType.DMA
    return pl.pallas_call(
        functools.partial(partial_sums, parts, subs),
        out_shape=jax.ShapeDtypeStruct((1, 3, rows * parts, lanes), jnp.bfloat16),
        in_specs=[pl.BlockSpec(memory_space=pltpu.VMEM)] * 2,
        out_specs=pl.BlockSpec(memory_space=pltpu.VMEM),
        scratch_shapes=[
            pltpu.VMEM((parts, rows, width), jnp.bfloat16),
            pltpu.VMEM(box, jnp.bfloat16),
            pltpu.VMEM(box, jnp.bfloat16),
            pltpu.VMEM(box, jnp.bfloat16),
            pltpu.VMEM((rows, 3 * lanes), jnp.float32),
            dma((4, 2)),
            dma((4, 2)),
            dma((parts, parts)),
            dma((parts, parts)),
            dma((parts, parts)),
        ],
        compiler_params=pltpu.CompilerParams(
            collective_id=0, has_side_effects=True, vmem_limit_bytes=48 * 2**20
        ),
    )(inputs, weight)


def fast_shards(token_ids, residual_in, embedding, in_weight, short_filter, decay_rate, residue, skip):
    tok_rows, width = residual_in.shape
    vocab_size = embedding.shape[0]
    channels = skip.shape[0]
    seq_parts = lax.axis_size("seq")
    me = lax.axis_index("seq")
    lanes = channels // seq_parts
    total = tok_rows * seq_parts
    onehot = (token_ids[:, None] == jnp.arange(vocab_size, dtype=jnp.int32)[None, :]).astype(jnp.bfloat16)
    embedded = jnp.dot(onehot, embedding, preferred_element_type=jnp.float32)
    inputs = (residual_in.astype(jnp.float32) + embedded).astype(jnp.bfloat16)
    weight = in_weight.transpose(1, 0, 2)
    partial = summed(inputs, weight, seq_parts, lax.axis_size("sub"))

    def own(x):
        return lax.dynamic_slice_in_dim(x, me * lanes, lanes, axis=x.ndim - 1)

    mixed = convolved(partial, own(short_filter), own(decay_rate), own(residue), own(skip))
    return lax.all_to_all(mixed, "seq", split_axis=0, concat_axis=1, tiled=True)


def fits(mesh):
    seq_parts = mesh.shape["seq"]
    return mesh.shape["ch"] == 2 and mesh.shape["sub"] == 2 and seq_parts == mesh.shape["ch"] * mesh.shape["sub"]


def solution(mesh):
    return jax.shard_map(
        fast_shards if fits(mesh) else shards,
        mesh=mesh,
        in_specs=(
            P(("grp", "seq")),
            P(("grp", "seq"), ("ch", "sub")),
            P(None, ("ch", "sub")),
            P("seq", None, ("ch", "sub")),
            P(None, None, ("ch", "sub")),
            P(None, ("ch", "sub")),
            P(None, ("ch", "sub")),
            P(("ch", "sub")),
        ),
        out_specs=P(("grp", "seq"), ("ch", "sub")),
        check_vma=False,
    )
```

```python
import functools

import jax
import jax.numpy as jnp
from jax import lax
from jax.experimental import pallas as pl
from jax.experimental.pallas import tpu as pltpu
from jax.sharding import PartitionSpec as P

PRECISE = lax.Precision.HIGHEST
TWO_PI = 6.283185307179586


def shifted(x, axis, by):
    peers = lax.axis_size(axis)
    pairs = [(i, i + by) for i in range(peers) if 0 <= i + by < peers]
    return lax.ppermute(x, axis, pairs)


def swapped(value, axis, apart):
    mask = 2**apart
    pairs = [(source, source ^ mask) for source in range(lax.axis_size(axis))]
    return lax.ppermute(value, axis, pairs)


def reversed_bits(number, bit_count):
    result = jnp.zeros_like(number)
    for section_bit in range(bit_count):
        result = result + (number >> section_bit & 1) * (1 << bit_count - 1 - section_bit)
    return result


def angle_table(left_idx, right_idx, period):
    wrapped = left_idx[:, None] * right_idx[None, :] % period
    return TWO_PI * wrapped.astype(jnp.float32) / period


def complex_mix(mat_re, mat_im, data_re, data_im):
    real_part = jnp.einsum("kr,rjc->kjc", mat_re, data_re, precision=PRECISE) - jnp.einsum(
        "kr,rjc->kjc", mat_im, data_im, precision=PRECISE
    )
    imag_part = jnp.einsum("kr,rjc->kjc", mat_re, data_im, precision=PRECISE) + jnp.einsum(
        "kr,rjc->kjc", mat_im, data_re, precision=PRECISE
    )
    return (real_part, imag_part)


def complex_dot(mat_re, mat_im, data_re, data_im):
    real_part = jnp.dot(mat_re, data_re, precision=PRECISE) - jnp.dot(
        mat_im, data_im, precision=PRECISE
    )
    imag_part = jnp.dot(mat_re, data_im, precision=PRECISE) + jnp.dot(
        mat_im, data_re, precision=PRECISE
    )
    return (real_part, imag_part)


def shards(token_ids, residual_in, embedding, in_weight, short_filter, decay_rate, residue, skip):
    tok_rows = residual_in.shape[0]
    vocab_size = embedding.shape[0]
    channels = skip.shape[0]
    seq_parts = lax.axis_size("seq")
    bit_count = seq_parts.bit_length() - 1
    my_index = lax.axis_index("seq")
    length = tok_rows * seq_parts
    padded_len = 2 * length
    group_rows = tok_rows // seq_parts
    onehot = (token_ids[:, None] == jnp.arange(vocab_size, dtype=jnp.int32)[None, :]).astype(
        jnp.bfloat16
    )
    embedded = jnp.dot(onehot, embedding, preferred_element_type=jnp.float32)
    inputs = (residual_in.astype(jnp.float32) + embedded).astype(jnp.bfloat16)
    features = lax.all_gather(inputs, ("ch", "sub"), axis=1, tiled=True)
    piece_rows = lax.all_gather(in_weight, "seq", axis=0, tiled=True)
    flat_piece = piece_rows.reshape(piece_rows.shape[0], 3 * channels)
    projected = jnp.dot(features, flat_piece, preferred_element_type=jnp.float32)
    projected = projected.astype(jnp.bfloat16).reshape(tok_rows, 3, channels)
    rim_rows = shifted(projected[tok_rows - 2 :], "seq", 1)
    extended = jnp.concatenate([rim_rows, projected], axis=0).astype(jnp.float32)
    mixed_in = (
        short_filter[0] * extended[2:]
        + short_filter[1] * extended[1:-1]
        + short_filter[2] * extended[:-2]
    )
    query_gate = mixed_in[:, 0]
    product = (mixed_in[:, 1] * mixed_in[:, 2]).astype(jnp.bfloat16)
    local_pos = jnp.arange(tok_rows, dtype=jnp.int32)
    sources = jnp.arange(seq_parts, dtype=jnp.int32)
    within_rows = my_index * group_rows + jnp.arange(group_rows, dtype=jnp.int32)
    block_pos = sources[:, None] * tok_rows + within_rows[None, :]
    block_angle = TWO_PI * block_pos.astype(jnp.float32) / padded_len
    pos_angle = TWO_PI * (my_index * tok_rows + local_pos).astype(jnp.float32) / padded_len
    values = product.astype(jnp.float32)
    state_re = jnp.concatenate([values, values * jnp.cos(pos_angle)[:, None]], -1)
    state_im = jnp.concatenate([jnp.zeros_like(values), -values * jnp.sin(pos_angle)[:, None]], -1)
    state_now = jnp.stack([state_re, state_im])
    for section_bit in range(bit_count - 1, -1, -1):
        half_span = 1 << section_bit
        partner = swapped(state_now.astype(jnp.bfloat16), "seq", section_bit).astype(
            state_now.dtype
        )
        upper_half = my_index >> section_bit & 1 == 1
        phase_now = TWO_PI * (my_index % half_span).astype(jnp.float32) / (2 * half_span)
        difference = partner - state_now
        rot_re = difference[0] * jnp.cos(phase_now) + difference[1] * jnp.sin(phase_now)
        rot_im = difference[1] * jnp.cos(phase_now) - difference[0] * jnp.sin(phase_now)
        state_now = jnp.where(upper_half, jnp.stack([rot_re, rot_im]), state_now + partner)
    own_freq = reversed_bits(my_index, bit_count)
    holders = reversed_bits(sources, bit_count)
    twist_angle = TWO_PI * (local_pos * own_freq % length).astype(jnp.float32) / length
    twist_re = jnp.cos(twist_angle)[:, None]
    twist_im = -jnp.sin(twist_angle)[:, None]
    spec_re = state_now[0] * twist_re - state_now[1] * twist_im
    spec_im = state_now[0] * twist_im + state_now[1] * twist_re
    kernel_table = angle_table(local_pos, local_pos, tok_rows)
    dft_re = jnp.cos(kernel_table)
    dft_im = -jnp.sin(kernel_table)
    spec_re, spec_im = complex_dot(dft_re, dft_im, spec_re, spec_im)
    parity = (jnp.arange(2 * channels, dtype=jnp.int32) >= channels).astype(jnp.int32)
    full_freq = 2 * (own_freq + seq_parts * local_pos)[:, None] + parity[None, :]
    freq_angle = TWO_PI * full_freq.astype(jnp.float32) / padded_len
    half_sine = jnp.sin(0.5 * freq_angle)
    sine_full = jnp.sin(freq_angle)
    sign_flip = 1.0 - 2.0 * parity.astype(jnp.float32)
    rates_both = jnp.concatenate([decay_rate, decay_rate], -1)
    residues_both = jnp.concatenate([residue, residue], -1)
    filt_re = jnp.zeros_like(spec_re)
    filt_im = jnp.zeros_like(spec_re)
    for mode_index in range(rates_both.shape[0]):
        rate_now = rates_both[mode_index]
        decay_now = jnp.exp(-rate_now)
        numerator = residues_both[mode_index] * (1.0 - sign_flip * jnp.exp(-rate_now * length))
        denom_re = -jnp.expm1(-rate_now) + 2.0 * decay_now * half_sine * half_sine
        denom_im = decay_now * sine_full
        scaled = numerator / (denom_re * denom_re + denom_im * denom_im)
        filt_re = filt_re + scaled * denom_re
        filt_im = filt_im - scaled * denom_im
    prod_re = spec_re * filt_re - spec_im * filt_im
    prod_im = spec_re * filt_im + spec_im * filt_re
    inv_re, inv_im = complex_dot(dft_re, -dft_im, prod_re, prod_im)
    back_re = inv_re * twist_re + inv_im * twist_im
    back_im = inv_im * twist_re - inv_re * twist_im
    returned = lax.all_to_all(
        jnp.stack([back_re, back_im]).reshape(2, 1, tok_rows, 2 * channels).astype(jnp.bfloat16),
        "seq",
        split_axis=2,
        concat_axis=1,
        tiled=True,
    ).astype(jnp.float32)
    inverse_angle = angle_table(sources, holders, seq_parts)
    block_re, block_im = complex_mix(
        jnp.cos(inverse_angle), jnp.sin(inverse_angle), returned[0], returned[1]
    )
    conv_blocks = (
        block_re[..., :channels]
        + jnp.cos(block_angle)[:, :, None] * block_re[..., channels:]
        - jnp.sin(block_angle)[:, :, None] * block_im[..., channels:]
    )
    conv_blocks = conv_blocks / padded_len
    conv_rows = lax.all_to_all(conv_blocks, "seq", split_axis=0, concat_axis=1, tiled=True)[0]
    mixed_out = (query_gate * (conv_rows + skip * product.astype(jnp.float32))).astype(jnp.bfloat16)
    return mixed_out


def mix_and_scan(rows, modes, part_ref, taps_ref, rate_ref, residue_ref, skip_ref, out_ref, proj, values, gate, result):
    total, lanes = out_ref.shape
    lead = proj.shape[1] - total
    at = pl.ds(pl.multiple_of(lax.axis_index("seq") * lanes, lanes), lanes)
    rates = rate_ref[:, at]
    weights = residue_ref[:, at]
    taps_count = taps_ref.shape[0]
    span = total // rows
    for g in range(3):
        proj[g, :lead, :] = jnp.zeros((lead, lanes), jnp.float32)
    parts = part_ref.shape[0]

    @pl.loop(0, 3)
    def _(g):
        acc = part_ref[0, g].astype(jnp.float32)
        for i in range(1, parts):
            acc = acc + part_ref[i, g].astype(jnp.float32)
        proj[g, lead:, :] = acc.astype(jnp.bfloat16).astype(jnp.float32)

    mixed = []
    for g in range(3):
        acc = None
        for i in range(taps_count):
            term = taps_ref[i, g : g + 1, at] * proj[g, pl.ds(lead - i, total), :]
            acc = term if acc is None else acc + term
        if g == 0:
            gate[...] = acc
        else:
            mixed.append(acc)
    values[...] = (mixed[0] * mixed[1]).astype(jnp.bfloat16).astype(jnp.float32)

    decay = [jnp.broadcast_to(jnp.exp(-rates[m : m + 1, :]), (rows, lanes)) for m in range(modes)]
    zero = jnp.zeros((rows, lanes), jnp.float32)

    def ends(j, state):
        now = values[pl.ds(j, rows, stride=span), :]
        return tuple(u * d + now for u, d in zip(state, decay))

    state = lax.fori_loop(0, span, ends, (zero,) * modes, unroll=4)
    index = lax.broadcasted_iota(jnp.int32, (rows, lanes), 0)

    def down(x, by):
        return jnp.where(index >= by, pltpu.roll(x, by, 0), 0.0)

    entering = []
    for m in range(modes):
        carry = down(state[m], 1)
        by = 1
        while by < rows:
            carry = carry + jnp.exp(-rates[m : m + 1, :] * (span * by)) * down(carry, by)
            by *= 2
        entering.append(carry)
    weight = [jnp.broadcast_to(weights[m : m + 1, :], (rows, lanes)) for m in range(modes)]
    direct = jnp.broadcast_to(skip_ref[:, at], (rows, lanes))

    def scan(j, state):
        here = pl.ds(j, rows, stride=span)
        now = values[here, :]
        state = tuple(u * d + now for u, d in zip(state, decay))
        terms = [u * w for u, w in zip(state, weight)] + [direct * now]
        while len(terms) > 1:
            terms = [a + b for a, b in zip(terms[::2], terms[1::2])] + terms[len(terms) // 2 * 2 :]
        result[here, :] = gate[here, :] * terms[0]
        return state

    lax.fori_loop(0, span, scan, tuple(entering), unroll=4)
    out_ref[...] = result[...].astype(out_ref.dtype)


def convolved(partial, short_filter, decay_rate, residue, skip):
    parts, _, total, lanes = partial.shape
    modes = decay_rate.shape[0]
    rows = 8
    f32 = jnp.float32
    return pl.pallas_call(
        functools.partial(mix_and_scan, rows, modes),
        out_shape=jax.ShapeDtypeStruct((total, lanes), jnp.bfloat16),
        in_specs=[pl.BlockSpec(memory_space=pltpu.VMEM)] * 5,
        out_specs=pl.BlockSpec(memory_space=pltpu.VMEM),
        scratch_shapes=[
            pltpu.VMEM((3, total + 8, lanes), f32),
            pltpu.VMEM((total, lanes), f32),
            pltpu.VMEM((total, lanes), f32),
            pltpu.VMEM((total, lanes), f32),
        ],
        compiler_params=pltpu.CompilerParams(vmem_limit_bytes=40 * 2**20),
    )(partial, short_filter, decay_rate, residue, skip.reshape(1, -1))


MESH = pl.DeviceIdType.MESH


def partial_sums(parts, subs, x_ref, w_ref, out_ref, held, outbox, from_below, from_above, acc, x_send, x_recv, box_send, below_recv, above_recv):
    z = lax.axis_index("seq")
    ch = lax.axis_index("ch")
    sub = lax.axis_index("sub")
    k = ch * subs + sub
    rows = x_ref.shape[0]
    pieces = 4
    half = rows // pieces
    lanes = w_ref.shape[2] // parts
    above = {"seq": lax.rem(z + 1, parts)}
    below = {"seq": lax.rem(z + parts - 1, parts)}
    turned = {"seq": k, "ch": z // subs, "sub": lax.rem(z, subs)}
    mirrored = {"seq": k, "ch": 1 - z // subs, "sub": lax.rem(z, subs)}
    source = {"seq": (1 - ch) * subs + sub, "ch": z // subs, "sub": lax.rem(z, subs)}
    sibling = {"sub": 1 - sub}
    across = {"ch": 1 - ch}
    moves = k != z

    barrier = pltpu.get_barrier_semaphore()

    def greet(device):
        pl.semaphore_signal(barrier, inc=1, device_id=device, device_id_type=MESH)

    greet(sibling)
    greet(across)
    greet(mirrored)
    greet(source)

    @pl.when(moves)
    def _():
        greet(turned)

    @pl.when(z > 0)
    def _():
        greet(below)

    @pl.when(z < parts - 1)
    def _():
        greet(above)

    peers = 4 + moves.astype(jnp.int32) + (z > 0).astype(jnp.int32) + (z < parts - 1).astype(jnp.int32)
    pl.semaphore_wait(barrier, peers)

    def piece(h):
        return pl.ds(h * half, half)

    def copy_x(kind, h, src, slot, device):
        return pltpu.make_async_remote_copy(
            src_ref=src,
            dst_ref=held.at[slot, piece(h)],
            send_sem=x_send.at[kind, h],
            recv_sem=x_recv.at[kind, h],
            device_id=device,
            device_id_type=MESH,
        )

    k_sibling = ch * subs + 1 - sub
    k_across = (1 - ch) * subs + sub
    k_far = (1 - ch) * subs + 1 - sub
    slots = [(k, k_across, k_sibling, k_far), (k_across, k, k_far, k_sibling)]

    @pl.when(moves)
    def _():
        for h in range(0, pieces, 2):
            copy_x(0, h, x_ref.at[piece(h)], z, turned).start()

    @pl.when(jnp.logical_not(moves))
    def _():
        for h in range(0, pieces, 2):
            pltpu.make_async_copy(x_ref.at[piece(h)], held.at[k, piece(h)], x_recv.at[0, h]).start()

    for h in range(1, pieces, 2):
        copy_x(0, h, x_ref.at[piece(h)], z, mirrored).start()

    for h in range(pieces):
        mine = slots[h % 2][0]
        if h % 2:
            copy_x(0, h, x_ref.at[piece(h)], mine, mirrored).wait_recv()
        else:
            @pl.when(moves)
            def _():
                copy_x(0, h, x_ref.at[piece(h)], mine, turned).wait_recv()

            @pl.when(jnp.logical_not(moves))
            def _():
                pltpu.make_async_copy(x_ref.at[piece(h)], held.at[mine, piece(h)], x_recv.at[0, h]).wait()

        copy_x(1, h, held.at[mine, piece(h)], mine, across).start()
        copy_x(2, h, held.at[mine, piece(h)], mine, sibling).start()
    for h in range(pieces):
        other = slots[h % 2][1]
        copy_x(1, h, held.at[other, piece(h)], other, across).wait_recv()
        copy_x(3, h, held.at[other, piece(h)], other, sibling).start()
    for h in range(pieces):
        copy_x(2, h, held.at[k, piece(h)], slots[h % 2][2], sibling).wait_recv()
        copy_x(3, h, held.at[k, piece(h)], slots[h % 2][3], sibling).wait_recv()

    def own(j, h):
        at = pl.ds(pl.multiple_of(j * lanes, lanes), lanes)
        columns = jnp.concatenate([w_ref[g, :, at] for g in range(3)], axis=1)
        acc[...] = jnp.dot(held[h], columns, preferred_element_type=jnp.float32)

    def rising(j, h):
        return pltpu.make_async_remote_copy(
            src_ref=outbox.at[j, h],
            dst_ref=from_below.at[j, h],
            send_sem=box_send.at[j, h],
            recv_sem=below_recv.at[j, h],
            device_id=above,
            device_id_type=MESH,
        )

    def falling(j, h):
        return pltpu.make_async_remote_copy(
            src_ref=outbox.at[j, h],
            dst_ref=from_above.at[j, h],
            send_sem=box_send.at[j, h],
            recv_sem=above_recv.at[j, h],
            device_id=below,
            device_id_type=MESH,
        )

    def add_below(j, h):
        @pl.when(z > 0)
        def _():
            rising(j, h).wait_recv()
            acc[...] += from_below[j, h].astype(jnp.float32)

    def add_above(j, h):
        @pl.when(z < parts - 1)
        def _():
            falling(j, h).wait_recv()
            acc[...] += from_above[j, h].astype(jnp.float32)

    def step(u, _):
        i = u // parts
        h = lax.rem(u, parts)
        up = parts - 1 - i

        @pl.when(up > z)
        def _():
            own(up, h)
            add_below(up, h)
            outbox[up, h] = acc[...].astype(jnp.bfloat16)
            rising(up, h).start()

        @pl.when(i < z)
        def _():
            own(i, h)
            add_above(i, h)
            outbox[i, h] = acc[...].astype(jnp.bfloat16)
            falling(i, h).start()

        return 0

    lax.fori_loop(0, (parts - 1) * parts, step, 0)

    def last(h, _):
        own(z, h)
        add_below(z, h)
        add_above(z, h)
        for g in range(3):
            out_ref[0, g, pl.ds(pl.multiple_of(h * rows, rows), rows), :] = acc[:, g * lanes : (g + 1) * lanes].astype(jnp.bfloat16)
        return 0

    lax.fori_loop(0, parts, last, 0)

    def drain(u, _):
        j = u // parts
        h = lax.rem(u, parts)

        @pl.when(j != z)
        def _():
            rising(j, h).wait_send()

        return 0

    lax.fori_loop(0, parts * parts, drain, 0)

    @pl.when(moves)
    def _():
        for h in range(0, pieces, 2):
            copy_x(0, h, x_ref.at[piece(h)], z, turned).wait_send()

    for h in range(1, pieces, 2):
        copy_x(0, h, x_ref.at[piece(h)], z, mirrored).wait_send()
    for h in range(pieces):
        for kind in (1, 2, 3):
            copy_x(kind, h, held.at[k, piece(h)], k, sibling).wait_send()


def summed(inputs, weight, parts, subs):
    rows, width = inputs.shape
    lanes = weight.shape[2] // parts
    box = (parts, parts, rows, 3 * lanes)
    dma = pltpu.SemaphoreType.DMA
    return pl.pallas_call(
        functools.partial(partial_sums, parts, subs),
        out_shape=jax.ShapeDtypeStruct((1, 3, rows * parts, lanes), jnp.bfloat16),
        in_specs=[pl.BlockSpec(memory_space=pltpu.VMEM)] * 2,
        out_specs=pl.BlockSpec(memory_space=pltpu.VMEM),
        scratch_shapes=[
            pltpu.VMEM((parts, rows, width), jnp.bfloat16),
            pltpu.VMEM(box, jnp.bfloat16),
            pltpu.VMEM(box, jnp.bfloat16),
            pltpu.VMEM(box, jnp.bfloat16),
            pltpu.VMEM((rows, 3 * lanes), jnp.float32),
            dma((4, 4)),
            dma((4, 4)),
            dma((parts, parts)),
            dma((parts, parts)),
            dma((parts, parts)),
        ],
        compiler_params=pltpu.CompilerParams(
            collective_id=0, has_side_effects=True, vmem_limit_bytes=48 * 2**20
        ),
    )(inputs, weight)


def fast_shards(token_ids, residual_in, embedding, in_weight, short_filter, decay_rate, residue, skip):
    tok_rows, width = residual_in.shape
    vocab_size = embedding.shape[0]
    channels = skip.shape[0]
    seq_parts = lax.axis_size("seq")
    onehot = (token_ids[:, None] == jnp.arange(vocab_size, dtype=jnp.int32)[None, :]).astype(jnp.bfloat16)
    embedded = jnp.dot(onehot, embedding, preferred_element_type=jnp.float32)
    inputs = (residual_in.astype(jnp.float32) + embedded).astype(jnp.bfloat16)
    weight = in_weight.transpose(1, 0, 2)
    partial = summed(inputs, weight, seq_parts, lax.axis_size("sub"))

    mixed = convolved(partial, short_filter, decay_rate, residue, skip)
    return lax.all_to_all(mixed, "seq", split_axis=0, concat_axis=1, tiled=True)


def fits(mesh):
    seq_parts = mesh.shape["seq"]
    return mesh.shape["ch"] == 2 and mesh.shape["sub"] == 2 and seq_parts == mesh.shape["ch"] * mesh.shape["sub"]


def solution(mesh):
    return jax.shard_map(
        fast_shards if fits(mesh) else shards,
        mesh=mesh,
        in_specs=(
            P(("grp", "seq")),
            P(("grp", "seq"), ("ch", "sub")),
            P(None, ("ch", "sub")),
            P("seq", None, ("ch", "sub")),
            P(None, None, ("ch", "sub")),
            P(None, ("ch", "sub")),
            P(None, ("ch", "sub")),
            P(("ch", "sub")),
        ),
        out_specs=P(("grp", "seq"), ("ch", "sub")),
        check_vma=False,
    )
```

```python
import functools

import jax
import jax.numpy as jnp
from jax import lax
from jax.experimental import pallas as pl
from jax.experimental.pallas import tpu as pltpu
from jax.sharding import PartitionSpec as P

PRECISE = lax.Precision.HIGHEST
TWO_PI = 6.283185307179586


def shifted(x, axis, by):
    peers = lax.axis_size(axis)
    pairs = [(i, i + by) for i in range(peers) if 0 <= i + by < peers]
    return lax.ppermute(x, axis, pairs)


def swapped(value, axis, apart):
    mask = 2**apart
    pairs = [(source, source ^ mask) for source in range(lax.axis_size(axis))]
    return lax.ppermute(value, axis, pairs)


def reversed_bits(number, bit_count):
    result = jnp.zeros_like(number)
    for section_bit in range(bit_count):
        result = result + (number >> section_bit & 1) * (1 << bit_count - 1 - section_bit)
    return result


def angle_table(left_idx, right_idx, period):
    wrapped = left_idx[:, None] * right_idx[None, :] % period
    return TWO_PI * wrapped.astype(jnp.float32) / period


def complex_mix(mat_re, mat_im, data_re, data_im):
    real_part = jnp.einsum("kr,rjc->kjc", mat_re, data_re, precision=PRECISE) - jnp.einsum(
        "kr,rjc->kjc", mat_im, data_im, precision=PRECISE
    )
    imag_part = jnp.einsum("kr,rjc->kjc", mat_re, data_im, precision=PRECISE) + jnp.einsum(
        "kr,rjc->kjc", mat_im, data_re, precision=PRECISE
    )
    return (real_part, imag_part)


def complex_dot(mat_re, mat_im, data_re, data_im):
    real_part = jnp.dot(mat_re, data_re, precision=PRECISE) - jnp.dot(
        mat_im, data_im, precision=PRECISE
    )
    imag_part = jnp.dot(mat_re, data_im, precision=PRECISE) + jnp.dot(
        mat_im, data_re, precision=PRECISE
    )
    return (real_part, imag_part)


def shards(token_ids, residual_in, embedding, in_weight, short_filter, decay_rate, residue, skip):
    tok_rows = residual_in.shape[0]
    vocab_size = embedding.shape[0]
    channels = skip.shape[0]
    seq_parts = lax.axis_size("seq")
    bit_count = seq_parts.bit_length() - 1
    my_index = lax.axis_index("seq")
    length = tok_rows * seq_parts
    padded_len = 2 * length
    group_rows = tok_rows // seq_parts
    onehot = (token_ids[:, None] == jnp.arange(vocab_size, dtype=jnp.int32)[None, :]).astype(
        jnp.bfloat16
    )
    embedded = jnp.dot(onehot, embedding, preferred_element_type=jnp.float32)
    inputs = (residual_in.astype(jnp.float32) + embedded).astype(jnp.bfloat16)
    features = lax.all_gather(inputs, ("ch", "sub"), axis=1, tiled=True)
    piece_rows = lax.all_gather(in_weight, "seq", axis=0, tiled=True)
    flat_piece = piece_rows.reshape(piece_rows.shape[0], 3 * channels)
    projected = jnp.dot(features, flat_piece, preferred_element_type=jnp.float32)
    projected = projected.astype(jnp.bfloat16).reshape(tok_rows, 3, channels)
    rim_rows = shifted(projected[tok_rows - 2 :], "seq", 1)
    extended = jnp.concatenate([rim_rows, projected], axis=0).astype(jnp.float32)
    mixed_in = (
        short_filter[0] * extended[2:]
        + short_filter[1] * extended[1:-1]
        + short_filter[2] * extended[:-2]
    )
    query_gate = mixed_in[:, 0]
    product = (mixed_in[:, 1] * mixed_in[:, 2]).astype(jnp.bfloat16)
    local_pos = jnp.arange(tok_rows, dtype=jnp.int32)
    sources = jnp.arange(seq_parts, dtype=jnp.int32)
    within_rows = my_index * group_rows + jnp.arange(group_rows, dtype=jnp.int32)
    block_pos = sources[:, None] * tok_rows + within_rows[None, :]
    block_angle = TWO_PI * block_pos.astype(jnp.float32) / padded_len
    pos_angle = TWO_PI * (my_index * tok_rows + local_pos).astype(jnp.float32) / padded_len
    values = product.astype(jnp.float32)
    state_re = jnp.concatenate([values, values * jnp.cos(pos_angle)[:, None]], -1)
    state_im = jnp.concatenate([jnp.zeros_like(values), -values * jnp.sin(pos_angle)[:, None]], -1)
    state_now = jnp.stack([state_re, state_im])
    for section_bit in range(bit_count - 1, -1, -1):
        half_span = 1 << section_bit
        partner = swapped(state_now.astype(jnp.bfloat16), "seq", section_bit).astype(
            state_now.dtype
        )
        upper_half = my_index >> section_bit & 1 == 1
        phase_now = TWO_PI * (my_index % half_span).astype(jnp.float32) / (2 * half_span)
        difference = partner - state_now
        rot_re = difference[0] * jnp.cos(phase_now) + difference[1] * jnp.sin(phase_now)
        rot_im = difference[1] * jnp.cos(phase_now) - difference[0] * jnp.sin(phase_now)
        state_now = jnp.where(upper_half, jnp.stack([rot_re, rot_im]), state_now + partner)
    own_freq = reversed_bits(my_index, bit_count)
    holders = reversed_bits(sources, bit_count)
    twist_angle = TWO_PI * (local_pos * own_freq % length).astype(jnp.float32) / length
    twist_re = jnp.cos(twist_angle)[:, None]
    twist_im = -jnp.sin(twist_angle)[:, None]
    spec_re = state_now[0] * twist_re - state_now[1] * twist_im
    spec_im = state_now[0] * twist_im + state_now[1] * twist_re
    kernel_table = angle_table(local_pos, local_pos, tok_rows)
    dft_re = jnp.cos(kernel_table)
    dft_im = -jnp.sin(kernel_table)
    spec_re, spec_im = complex_dot(dft_re, dft_im, spec_re, spec_im)
    parity = (jnp.arange(2 * channels, dtype=jnp.int32) >= channels).astype(jnp.int32)
    full_freq = 2 * (own_freq + seq_parts * local_pos)[:, None] + parity[None, :]
    freq_angle = TWO_PI * full_freq.astype(jnp.float32) / padded_len
    half_sine = jnp.sin(0.5 * freq_angle)
    sine_full = jnp.sin(freq_angle)
    sign_flip = 1.0 - 2.0 * parity.astype(jnp.float32)
    rates_both = jnp.concatenate([decay_rate, decay_rate], -1)
    residues_both = jnp.concatenate([residue, residue], -1)
    filt_re = jnp.zeros_like(spec_re)
    filt_im = jnp.zeros_like(spec_re)
    for mode_index in range(rates_both.shape[0]):
        rate_now = rates_both[mode_index]
        decay_now = jnp.exp(-rate_now)
        numerator = residues_both[mode_index] * (1.0 - sign_flip * jnp.exp(-rate_now * length))
        denom_re = -jnp.expm1(-rate_now) + 2.0 * decay_now * half_sine * half_sine
        denom_im = decay_now * sine_full
        scaled = numerator / (denom_re * denom_re + denom_im * denom_im)
        filt_re = filt_re + scaled * denom_re
        filt_im = filt_im - scaled * denom_im
    prod_re = spec_re * filt_re - spec_im * filt_im
    prod_im = spec_re * filt_im + spec_im * filt_re
    inv_re, inv_im = complex_dot(dft_re, -dft_im, prod_re, prod_im)
    back_re = inv_re * twist_re + inv_im * twist_im
    back_im = inv_im * twist_re - inv_re * twist_im
    returned = lax.all_to_all(
        jnp.stack([back_re, back_im]).reshape(2, 1, tok_rows, 2 * channels).astype(jnp.bfloat16),
        "seq",
        split_axis=2,
        concat_axis=1,
        tiled=True,
    ).astype(jnp.float32)
    inverse_angle = angle_table(sources, holders, seq_parts)
    block_re, block_im = complex_mix(
        jnp.cos(inverse_angle), jnp.sin(inverse_angle), returned[0], returned[1]
    )
    conv_blocks = (
        block_re[..., :channels]
        + jnp.cos(block_angle)[:, :, None] * block_re[..., channels:]
        - jnp.sin(block_angle)[:, :, None] * block_im[..., channels:]
    )
    conv_blocks = conv_blocks / padded_len
    conv_rows = lax.all_to_all(conv_blocks, "seq", split_axis=0, concat_axis=1, tiled=True)[0]
    mixed_out = (query_gate * (conv_rows + skip * product.astype(jnp.float32))).astype(jnp.bfloat16)
    return mixed_out


def mix_and_scan(rows, modes, part_ref, taps_ref, rate_ref, residue_ref, skip_ref, out_ref, proj, values, gate, result):
    total, lanes = out_ref.shape
    lead = proj.shape[1] - total
    at = pl.ds(pl.multiple_of(lax.axis_index("seq") * lanes, lanes), lanes)
    rates = rate_ref[:, at]
    weights = residue_ref[:, at]
    taps_count = taps_ref.shape[0]
    span = total // rows
    for g in range(3):
        proj[g, :lead, :] = jnp.zeros((lead, lanes), jnp.float32)
    parts = part_ref.shape[0]

    @pl.loop(0, 3)
    def _(g):
        acc = part_ref[0, g].astype(jnp.float32)
        for i in range(1, parts):
            acc = acc + part_ref[i, g].astype(jnp.float32)
        proj[g, lead:, :] = acc.astype(jnp.bfloat16).astype(jnp.float32)

    mixed = []
    for g in range(3):
        acc = None
        for i in range(taps_count):
            term = taps_ref[i, g : g + 1, at] * proj[g, pl.ds(lead - i, total), :]
            acc = term if acc is None else acc + term
        if g == 0:
            gate[...] = acc
        else:
            mixed.append(acc)
    values[...] = (mixed[0] * mixed[1]).astype(jnp.bfloat16).astype(jnp.float32)

    decay = [jnp.broadcast_to(jnp.exp(-rates[m : m + 1, :]), (rows, lanes)) for m in range(modes)]
    zero = jnp.zeros((rows, lanes), jnp.float32)

    def ends(j, state):
        now = values[pl.ds(j, rows, stride=span), :]
        return tuple(u * d + now for u, d in zip(state, decay))

    state = lax.fori_loop(0, span, ends, (zero,) * modes, unroll=4)
    index = lax.broadcasted_iota(jnp.int32, (rows, lanes), 0)

    def down(x, by):
        return jnp.where(index >= by, pltpu.roll(x, by, 0), 0.0)

    entering = []
    for m in range(modes):
        carry = down(state[m], 1)
        by = 1
        while by < rows:
            carry = carry + jnp.exp(-rates[m : m + 1, :] * (span * by)) * down(carry, by)
            by *= 2
        entering.append(carry)
    weight = [jnp.broadcast_to(weights[m : m + 1, :], (rows, lanes)) for m in range(modes)]
    direct = jnp.broadcast_to(skip_ref[:, at], (rows, lanes))

    def scan(j, state):
        here = pl.ds(j, rows, stride=span)
        now = values[here, :]
        state = tuple(u * d + now for u, d in zip(state, decay))
        terms = [u * w for u, w in zip(state, weight)] + [direct * now]
        while len(terms) > 1:
            terms = [a + b for a, b in zip(terms[::2], terms[1::2])] + terms[len(terms) // 2 * 2 :]
        result[here, :] = gate[here, :] * terms[0]
        return state

    lax.fori_loop(0, span, scan, tuple(entering), unroll=4)
    out_ref[...] = result[...].astype(out_ref.dtype)


def convolved(partial, short_filter, decay_rate, residue, skip):
    parts, _, total, lanes = partial.shape
    modes = decay_rate.shape[0]
    rows = 8
    f32 = jnp.float32
    return pl.pallas_call(
        functools.partial(mix_and_scan, rows, modes),
        out_shape=jax.ShapeDtypeStruct((total, lanes), jnp.bfloat16),
        in_specs=[pl.BlockSpec(memory_space=pltpu.VMEM)] * 5,
        out_specs=pl.BlockSpec(memory_space=pltpu.VMEM),
        scratch_shapes=[
            pltpu.VMEM((3, total + 8, lanes), f32),
            pltpu.VMEM((total, lanes), f32),
            pltpu.VMEM((total, lanes), f32),
            pltpu.VMEM((total, lanes), f32),
        ],
        compiler_params=pltpu.CompilerParams(vmem_limit_bytes=40 * 2**20),
    )(partial, short_filter, decay_rate, residue, skip.reshape(1, -1))


MESH = pl.DeviceIdType.MESH


def partial_sums(parts, subs, x_ref, w_ref, out_ref, held, outbox, from_below, from_above, acc, x_send, x_recv, box_send, below_recv, above_recv):
    z = lax.axis_index("seq")
    ch = lax.axis_index("ch")
    sub = lax.axis_index("sub")
    k = ch * subs + sub
    rows = x_ref.shape[0]
    pieces = 4
    half = rows // pieces
    lanes = w_ref.shape[2] // parts
    above = {"seq": lax.rem(z + 1, parts)}
    below = {"seq": lax.rem(z + parts - 1, parts)}
    turned = {"seq": k, "ch": z // subs, "sub": lax.rem(z, subs)}
    mirrored = {"seq": k, "ch": 1 - z // subs, "sub": lax.rem(z, subs)}
    source = {"seq": (1 - ch) * subs + sub, "ch": z // subs, "sub": lax.rem(z, subs)}
    sibling = {"sub": 1 - sub}
    across = {"ch": 1 - ch}
    moves = k != z

    barrier = pltpu.get_barrier_semaphore()

    def greet(device):
        pl.semaphore_signal(barrier, inc=1, device_id=device, device_id_type=MESH)

    greet(sibling)
    greet(across)
    greet(mirrored)
    greet(source)

    @pl.when(moves)
    def _():
        greet(turned)

    @pl.when(z > 0)
    def _():
        greet(below)

    @pl.when(z < parts - 1)
    def _():
        greet(above)

    peers = 4 + moves.astype(jnp.int32) + (z > 0).astype(jnp.int32) + (z < parts - 1).astype(jnp.int32)
    pl.semaphore_wait(barrier, peers)

    def piece(h):
        return pl.ds(h * half, half)

    def copy_x(kind, h, src, slot, device):
        return pltpu.make_async_remote_copy(
            src_ref=src,
            dst_ref=held.at[slot, piece(h)],
            send_sem=x_send.at[kind, h],
            recv_sem=x_recv.at[kind, h],
            device_id=device,
            device_id_type=MESH,
        )

    k_sibling = ch * subs + 1 - sub
    k_across = (1 - ch) * subs + sub
    k_far = (1 - ch) * subs + 1 - sub
    slots = [(k, k_across, k_sibling, k_far), (k_across, k, k_far, k_sibling)]

    @pl.when(moves)
    def _():
        for h in range(0, pieces, 2):
            copy_x(0, h, x_ref.at[piece(h)], z, turned).start()

    @pl.when(jnp.logical_not(moves))
    def _():
        for h in range(0, pieces, 2):
            pltpu.make_async_copy(x_ref.at[piece(h)], held.at[k, piece(h)], x_recv.at[0, h]).start()

    for h in range(1, pieces, 2):
        copy_x(0, h, x_ref.at[piece(h)], z, mirrored).start()

    for h in range(pieces):
        mine = slots[h % 2][0]
        if h % 2:
            copy_x(0, h, x_ref.at[piece(h)], mine, mirrored).wait_recv()
        else:
            @pl.when(moves)
            def _():
                copy_x(0, h, x_ref.at[piece(h)], mine, turned).wait_recv()

            @pl.when(jnp.logical_not(moves))
            def _():
                pltpu.make_async_copy(x_ref.at[piece(h)], held.at[mine, piece(h)], x_recv.at[0, h]).wait()

        copy_x(1, h, held.at[mine, piece(h)], mine, across).start()
        copy_x(2, h, held.at[mine, piece(h)], mine, sibling).start()
    for h in range(pieces):
        other = slots[h % 2][1]
        copy_x(1, h, held.at[other, piece(h)], other, across).wait_recv()
        copy_x(3, h, held.at[other, piece(h)], other, sibling).start()
    def block_at(q):
        return lax.rem(ch + q, 2) * subs + lax.rem(sub + q // 2, 2)

    def own(j, h):
        at = pl.ds(pl.multiple_of(j * lanes, lanes), lanes)
        columns = jnp.concatenate([w_ref[g, :, at] for g in range(3)], axis=1)
        acc[...] = jnp.dot(held[h], columns, preferred_element_type=jnp.float32)

    def rising(j, h):
        return pltpu.make_async_remote_copy(
            src_ref=outbox.at[j, h],
            dst_ref=from_below.at[j, h],
            send_sem=box_send.at[j, h],
            recv_sem=below_recv.at[j, h],
            device_id=above,
            device_id_type=MESH,
        )

    def falling(j, h):
        return pltpu.make_async_remote_copy(
            src_ref=outbox.at[j, h],
            dst_ref=from_above.at[j, h],
            send_sem=box_send.at[j, h],
            recv_sem=above_recv.at[j, h],
            device_id=below,
            device_id_type=MESH,
        )

    def add_below(j, h):
        @pl.when(z > 0)
        def _():
            rising(j, h).wait_recv()
            acc[...] += from_below[j, h].astype(jnp.float32)

    def add_above(j, h):
        @pl.when(z < parts - 1)
        def _():
            falling(j, h).wait_recv()
            acc[...] += from_above[j, h].astype(jnp.float32)

    def step(u, _):
        i = u // parts
        h = block_at(lax.rem(u, parts))
        up = parts - 1 - i

        @pl.when(u == 2)
        def _():
            for n in range(pieces):
                copy_x(2, n, held.at[k, piece(n)], slots[n % 2][2], sibling).wait_recv()
                copy_x(3, n, held.at[k, piece(n)], slots[n % 2][3], sibling).wait_recv()

        @pl.when(up > z)
        def _():
            own(up, h)
            add_below(up, h)
            outbox[up, h] = acc[...].astype(jnp.bfloat16)
            rising(up, h).start()

        @pl.when(i < z)
        def _():
            own(i, h)
            add_above(i, h)
            outbox[i, h] = acc[...].astype(jnp.bfloat16)
            falling(i, h).start()

        return 0

    lax.fori_loop(0, (parts - 1) * parts, step, 0)

    def last(q, _):
        h = block_at(q)
        own(z, h)
        add_below(z, h)
        add_above(z, h)
        for g in range(3):
            out_ref[0, g, pl.ds(pl.multiple_of(h * rows, rows), rows), :] = acc[:, g * lanes : (g + 1) * lanes].astype(jnp.bfloat16)
        return 0

    lax.fori_loop(0, parts, last, 0)

    def drain(u, _):
        j = u // parts
        h = lax.rem(u, parts)

        @pl.when(j != z)
        def _():
            rising(j, h).wait_send()

        return 0

    lax.fori_loop(0, parts * parts, drain, 0)

    @pl.when(moves)
    def _():
        for h in range(0, pieces, 2):
            copy_x(0, h, x_ref.at[piece(h)], z, turned).wait_send()

    for h in range(1, pieces, 2):
        copy_x(0, h, x_ref.at[piece(h)], z, mirrored).wait_send()
    for h in range(pieces):
        for kind in (1, 2, 3):
            copy_x(kind, h, held.at[k, piece(h)], k, sibling).wait_send()


def summed(inputs, weight, parts, subs):
    rows, width = inputs.shape
    lanes = weight.shape[2] // parts
    box = (parts, parts, rows, 3 * lanes)
    dma = pltpu.SemaphoreType.DMA
    return pl.pallas_call(
        functools.partial(partial_sums, parts, subs),
        out_shape=jax.ShapeDtypeStruct((1, 3, rows * parts, lanes), jnp.bfloat16),
        in_specs=[pl.BlockSpec(memory_space=pltpu.VMEM)] * 2,
        out_specs=pl.BlockSpec(memory_space=pltpu.VMEM),
        scratch_shapes=[
            pltpu.VMEM((parts, rows, width), jnp.bfloat16),
            pltpu.VMEM(box, jnp.bfloat16),
            pltpu.VMEM(box, jnp.bfloat16),
            pltpu.VMEM(box, jnp.bfloat16),
            pltpu.VMEM((rows, 3 * lanes), jnp.float32),
            dma((4, 4)),
            dma((4, 4)),
            dma((parts, parts)),
            dma((parts, parts)),
            dma((parts, parts)),
        ],
        compiler_params=pltpu.CompilerParams(
            collective_id=0, has_side_effects=True, vmem_limit_bytes=48 * 2**20
        ),
    )(inputs, weight)


def fast_shards(token_ids, residual_in, embedding, in_weight, short_filter, decay_rate, residue, skip):
    tok_rows, width = residual_in.shape
    vocab_size = embedding.shape[0]
    channels = skip.shape[0]
    seq_parts = lax.axis_size("seq")
    onehot = (token_ids[:, None] == jnp.arange(vocab_size, dtype=jnp.int32)[None, :]).astype(jnp.bfloat16)
    embedded = jnp.dot(onehot, embedding, preferred_element_type=jnp.float32)
    inputs = (residual_in.astype(jnp.float32) + embedded).astype(jnp.bfloat16)
    weight = in_weight.transpose(1, 0, 2)
    partial = summed(inputs, weight, seq_parts, lax.axis_size("sub"))

    mixed = convolved(partial, short_filter, decay_rate, residue, skip)
    return lax.all_to_all(mixed, "seq", split_axis=0, concat_axis=1, tiled=True)


def fits(mesh):
    seq_parts = mesh.shape["seq"]
    return mesh.shape["ch"] == 2 and mesh.shape["sub"] == 2 and seq_parts == mesh.shape["ch"] * mesh.shape["sub"]


def solution(mesh):
    return jax.shard_map(
        fast_shards if fits(mesh) else shards,
        mesh=mesh,
        in_specs=(
            P(("grp", "seq")),
            P(("grp", "seq"), ("ch", "sub")),
            P(None, ("ch", "sub")),
            P("seq", None, ("ch", "sub")),
            P(None, None, ("ch", "sub")),
            P(None, ("ch", "sub")),
            P(None, ("ch", "sub")),
            P(("ch", "sub")),
        ),
        out_specs=P(("grp", "seq"), ("ch", "sub")),
        check_vma=False,
    )
```

```python
import functools

import jax
import jax.numpy as jnp
from jax import lax
from jax.experimental import pallas as pl
from jax.experimental.pallas import tpu as pltpu
from jax.sharding import PartitionSpec as P

PRECISE = lax.Precision.HIGHEST
TWO_PI = 6.283185307179586


def shifted(x, axis, by):
    peers = lax.axis_size(axis)
    pairs = [(i, i + by) for i in range(peers) if 0 <= i + by < peers]
    return lax.ppermute(x, axis, pairs)


def swapped(value, axis, apart):
    mask = 2**apart
    pairs = [(source, source ^ mask) for source in range(lax.axis_size(axis))]
    return lax.ppermute(value, axis, pairs)


def reversed_bits(number, bit_count):
    result = jnp.zeros_like(number)
    for section_bit in range(bit_count):
        result = result + (number >> section_bit & 1) * (1 << bit_count - 1 - section_bit)
    return result


def angle_table(left_idx, right_idx, period):
    wrapped = left_idx[:, None] * right_idx[None, :] % period
    return TWO_PI * wrapped.astype(jnp.float32) / period


def complex_mix(mat_re, mat_im, data_re, data_im):
    real_part = jnp.einsum("kr,rjc->kjc", mat_re, data_re, precision=PRECISE) - jnp.einsum(
        "kr,rjc->kjc", mat_im, data_im, precision=PRECISE
    )
    imag_part = jnp.einsum("kr,rjc->kjc", mat_re, data_im, precision=PRECISE) + jnp.einsum(
        "kr,rjc->kjc", mat_im, data_re, precision=PRECISE
    )
    return (real_part, imag_part)


def complex_dot(mat_re, mat_im, data_re, data_im):
    real_part = jnp.dot(mat_re, data_re, precision=PRECISE) - jnp.dot(
        mat_im, data_im, precision=PRECISE
    )
    imag_part = jnp.dot(mat_re, data_im, precision=PRECISE) + jnp.dot(
        mat_im, data_re, precision=PRECISE
    )
    return (real_part, imag_part)


def shards(token_ids, residual_in, embedding, in_weight, short_filter, decay_rate, residue, skip):
    tok_rows = residual_in.shape[0]
    vocab_size = embedding.shape[0]
    channels = skip.shape[0]
    seq_parts = lax.axis_size("seq")
    bit_count = seq_parts.bit_length() - 1
    my_index = lax.axis_index("seq")
    length = tok_rows * seq_parts
    padded_len = 2 * length
    group_rows = tok_rows // seq_parts
    onehot = (token_ids[:, None] == jnp.arange(vocab_size, dtype=jnp.int32)[None, :]).astype(
        jnp.bfloat16
    )
    embedded = jnp.dot(onehot, embedding, preferred_element_type=jnp.float32)
    inputs = (residual_in.astype(jnp.float32) + embedded).astype(jnp.bfloat16)
    features = lax.all_gather(inputs, ("ch", "sub"), axis=1, tiled=True)
    piece_rows = lax.all_gather(in_weight, "seq", axis=0, tiled=True)
    flat_piece = piece_rows.reshape(piece_rows.shape[0], 3 * channels)
    projected = jnp.dot(features, flat_piece, preferred_element_type=jnp.float32)
    projected = projected.astype(jnp.bfloat16).reshape(tok_rows, 3, channels)
    rim_rows = shifted(projected[tok_rows - 2 :], "seq", 1)
    extended = jnp.concatenate([rim_rows, projected], axis=0).astype(jnp.float32)
    mixed_in = (
        short_filter[0] * extended[2:]
        + short_filter[1] * extended[1:-1]
        + short_filter[2] * extended[:-2]
    )
    query_gate = mixed_in[:, 0]
    product = (mixed_in[:, 1] * mixed_in[:, 2]).astype(jnp.bfloat16)
    local_pos = jnp.arange(tok_rows, dtype=jnp.int32)
    sources = jnp.arange(seq_parts, dtype=jnp.int32)
    within_rows = my_index * group_rows + jnp.arange(group_rows, dtype=jnp.int32)
    block_pos = sources[:, None] * tok_rows + within_rows[None, :]
    block_angle = TWO_PI * block_pos.astype(jnp.float32) / padded_len
    pos_angle = TWO_PI * (my_index * tok_rows + local_pos).astype(jnp.float32) / padded_len
    values = product.astype(jnp.float32)
    state_re = jnp.concatenate([values, values * jnp.cos(pos_angle)[:, None]], -1)
    state_im = jnp.concatenate([jnp.zeros_like(values), -values * jnp.sin(pos_angle)[:, None]], -1)
    state_now = jnp.stack([state_re, state_im])
    for section_bit in range(bit_count - 1, -1, -1):
        half_span = 1 << section_bit
        partner = swapped(state_now.astype(jnp.bfloat16), "seq", section_bit).astype(
            state_now.dtype
        )
        upper_half = my_index >> section_bit & 1 == 1
        phase_now = TWO_PI * (my_index % half_span).astype(jnp.float32) / (2 * half_span)
        difference = partner - state_now
        rot_re = difference[0] * jnp.cos(phase_now) + difference[1] * jnp.sin(phase_now)
        rot_im = difference[1] * jnp.cos(phase_now) - difference[0] * jnp.sin(phase_now)
        state_now = jnp.where(upper_half, jnp.stack([rot_re, rot_im]), state_now + partner)
    own_freq = reversed_bits(my_index, bit_count)
    holders = reversed_bits(sources, bit_count)
    twist_angle = TWO_PI * (local_pos * own_freq % length).astype(jnp.float32) / length
    twist_re = jnp.cos(twist_angle)[:, None]
    twist_im = -jnp.sin(twist_angle)[:, None]
    spec_re = state_now[0] * twist_re - state_now[1] * twist_im
    spec_im = state_now[0] * twist_im + state_now[1] * twist_re
    kernel_table = angle_table(local_pos, local_pos, tok_rows)
    dft_re = jnp.cos(kernel_table)
    dft_im = -jnp.sin(kernel_table)
    spec_re, spec_im = complex_dot(dft_re, dft_im, spec_re, spec_im)
    parity = (jnp.arange(2 * channels, dtype=jnp.int32) >= channels).astype(jnp.int32)
    full_freq = 2 * (own_freq + seq_parts * local_pos)[:, None] + parity[None, :]
    freq_angle = TWO_PI * full_freq.astype(jnp.float32) / padded_len
    half_sine = jnp.sin(0.5 * freq_angle)
    sine_full = jnp.sin(freq_angle)
    sign_flip = 1.0 - 2.0 * parity.astype(jnp.float32)
    rates_both = jnp.concatenate([decay_rate, decay_rate], -1)
    residues_both = jnp.concatenate([residue, residue], -1)
    filt_re = jnp.zeros_like(spec_re)
    filt_im = jnp.zeros_like(spec_re)
    for mode_index in range(rates_both.shape[0]):
        rate_now = rates_both[mode_index]
        decay_now = jnp.exp(-rate_now)
        numerator = residues_both[mode_index] * (1.0 - sign_flip * jnp.exp(-rate_now * length))
        denom_re = -jnp.expm1(-rate_now) + 2.0 * decay_now * half_sine * half_sine
        denom_im = decay_now * sine_full
        scaled = numerator / (denom_re * denom_re + denom_im * denom_im)
        filt_re = filt_re + scaled * denom_re
        filt_im = filt_im - scaled * denom_im
    prod_re = spec_re * filt_re - spec_im * filt_im
    prod_im = spec_re * filt_im + spec_im * filt_re
    inv_re, inv_im = complex_dot(dft_re, -dft_im, prod_re, prod_im)
    back_re = inv_re * twist_re + inv_im * twist_im
    back_im = inv_im * twist_re - inv_re * twist_im
    returned = lax.all_to_all(
        jnp.stack([back_re, back_im]).reshape(2, 1, tok_rows, 2 * channels).astype(jnp.bfloat16),
        "seq",
        split_axis=2,
        concat_axis=1,
        tiled=True,
    ).astype(jnp.float32)
    inverse_angle = angle_table(sources, holders, seq_parts)
    block_re, block_im = complex_mix(
        jnp.cos(inverse_angle), jnp.sin(inverse_angle), returned[0], returned[1]
    )
    conv_blocks = (
        block_re[..., :channels]
        + jnp.cos(block_angle)[:, :, None] * block_re[..., channels:]
        - jnp.sin(block_angle)[:, :, None] * block_im[..., channels:]
    )
    conv_blocks = conv_blocks / padded_len
    conv_rows = lax.all_to_all(conv_blocks, "seq", split_axis=0, concat_axis=1, tiled=True)[0]
    mixed_out = (query_gate * (conv_rows + skip * product.astype(jnp.float32))).astype(jnp.bfloat16)
    return mixed_out


def mix_and_scan(rows, modes, part_ref, taps_ref, rate_ref, residue_ref, skip_ref, out_ref, proj, values, gate, result):
    total, lanes = out_ref.shape
    lead = proj.shape[1] - total
    at = pl.ds(pl.multiple_of(lax.axis_index("seq") * lanes, lanes), lanes)
    rates = rate_ref[:, at]
    weights = residue_ref[:, at]
    taps_count = taps_ref.shape[0]
    span = total // rows
    for g in range(3):
        proj[g, :lead, :] = jnp.zeros((lead, lanes), jnp.float32)
    parts = part_ref.shape[0]

    @pl.loop(0, 3)
    def _(g):
        acc = part_ref[0, g].astype(jnp.float32)
        for i in range(1, parts):
            acc = acc + part_ref[i, g].astype(jnp.float32)
        proj[g, lead:, :] = acc.astype(jnp.bfloat16).astype(jnp.float32)

    mixed = []
    for g in range(3):
        acc = None
        for i in range(taps_count):
            term = taps_ref[i, g : g + 1, at] * proj[g, pl.ds(lead - i, total), :]
            acc = term if acc is None else acc + term
        if g == 0:
            gate[...] = acc
        else:
            mixed.append(acc)
    values[...] = (mixed[0] * mixed[1]).astype(jnp.bfloat16).astype(jnp.float32)

    decay = [jnp.broadcast_to(jnp.exp(-rates[m : m + 1, :]), (rows, lanes)) for m in range(modes)]
    zero = jnp.zeros((rows, lanes), jnp.float32)

    def ends(j, state):
        now = values[pl.ds(j, rows, stride=span), :]
        return tuple(u * d + now for u, d in zip(state, decay))

    state = lax.fori_loop(0, span, ends, (zero,) * modes, unroll=4)
    index = lax.broadcasted_iota(jnp.int32, (rows, lanes), 0)

    def down(x, by):
        return jnp.where(index >= by, pltpu.roll(x, by, 0), 0.0)

    entering = []
    for m in range(modes):
        carry = down(state[m], 1)
        by = 1
        while by < rows:
            carry = carry + jnp.exp(-rates[m : m + 1, :] * (span * by)) * down(carry, by)
            by *= 2
        entering.append(carry)
    weight = [jnp.broadcast_to(weights[m : m + 1, :], (rows, lanes)) for m in range(modes)]
    direct = jnp.broadcast_to(skip_ref[:, at], (rows, lanes))

    def scan(j, state):
        here = pl.ds(j, rows, stride=span)
        now = values[here, :]
        state = tuple(u * d + now for u, d in zip(state, decay))
        terms = [u * w for u, w in zip(state, weight)] + [direct * now]
        while len(terms) > 1:
            terms = [a + b for a, b in zip(terms[::2], terms[1::2])] + terms[len(terms) // 2 * 2 :]
        result[here, :] = gate[here, :] * terms[0]
        return state

    lax.fori_loop(0, span, scan, tuple(entering), unroll=4)
    out_ref[...] = result[...].astype(out_ref.dtype)


def convolved(partial, short_filter, decay_rate, residue, skip):
    parts, _, total, lanes = partial.shape
    modes = decay_rate.shape[0]
    rows = 8
    f32 = jnp.float32
    return pl.pallas_call(
        functools.partial(mix_and_scan, rows, modes),
        out_shape=jax.ShapeDtypeStruct((total, lanes), jnp.bfloat16),
        in_specs=[pl.BlockSpec(memory_space=pltpu.VMEM)] * 5,
        out_specs=pl.BlockSpec(memory_space=pltpu.VMEM),
        scratch_shapes=[
            pltpu.VMEM((3, total + 8, lanes), f32),
            pltpu.VMEM((total, lanes), f32),
            pltpu.VMEM((total, lanes), f32),
            pltpu.VMEM((total, lanes), f32),
        ],
        compiler_params=pltpu.CompilerParams(vmem_limit_bytes=40 * 2**20),
    )(partial, short_filter, decay_rate, residue, skip.reshape(1, -1))


MESH = pl.DeviceIdType.MESH


def partial_sums(parts, subs, x_ref, w_ref, out_ref, held, outbox, from_below, from_above, acc, x_send, x_recv, box_send, below_recv, above_recv):
    z = lax.axis_index("seq")
    ch = lax.axis_index("ch")
    sub = lax.axis_index("sub")
    k = ch * subs + sub
    rows = x_ref.shape[0]
    pieces = 8
    half = rows // pieces
    lanes = w_ref.shape[2] // parts
    above = {"seq": lax.rem(z + 1, parts)}
    below = {"seq": lax.rem(z + parts - 1, parts)}
    turned = {"seq": k, "ch": z // subs, "sub": lax.rem(z, subs)}
    mirrored = {"seq": k, "ch": 1 - z // subs, "sub": lax.rem(z, subs)}
    source = {"seq": (1 - ch) * subs + sub, "ch": z // subs, "sub": lax.rem(z, subs)}
    sibling = {"sub": 1 - sub}
    across = {"ch": 1 - ch}
    moves = k != z

    barrier = pltpu.get_barrier_semaphore()

    def greet(device):
        pl.semaphore_signal(barrier, inc=1, device_id=device, device_id_type=MESH)

    greet(sibling)
    greet(across)
    greet(mirrored)
    greet(source)

    @pl.when(moves)
    def _():
        greet(turned)

    @pl.when(z > 0)
    def _():
        greet(below)

    @pl.when(z < parts - 1)
    def _():
        greet(above)

    peers = 4 + moves.astype(jnp.int32) + (z > 0).astype(jnp.int32) + (z < parts - 1).astype(jnp.int32)
    pl.semaphore_wait(barrier, peers)

    def piece(h):
        return pl.ds(h * half, half)

    def copy_x(kind, h, src, slot, device):
        return pltpu.make_async_remote_copy(
            src_ref=src,
            dst_ref=held.at[slot, piece(h)],
            send_sem=x_send.at[kind, h],
            recv_sem=x_recv.at[kind, h],
            device_id=device,
            device_id_type=MESH,
        )

    k_sibling = ch * subs + 1 - sub
    k_across = (1 - ch) * subs + sub
    k_far = (1 - ch) * subs + 1 - sub
    slots = [(k, k_across, k_sibling, k_far), (k_across, k, k_far, k_sibling)]

    @pl.when(moves)
    def _():
        for h in range(0, pieces, 2):
            copy_x(0, h, x_ref.at[piece(h)], z, turned).start()

    @pl.when(jnp.logical_not(moves))
    def _():
        for h in range(0, pieces, 2):
            pltpu.make_async_copy(x_ref.at[piece(h)], held.at[k, piece(h)], x_recv.at[0, h]).start()

    for h in range(1, pieces, 2):
        copy_x(0, h, x_ref.at[piece(h)], z, mirrored).start()

    for h in range(pieces):
        mine = slots[h % 2][0]
        if h % 2:
            copy_x(0, h, x_ref.at[piece(h)], mine, mirrored).wait_recv()
        else:
            @pl.when(moves)
            def _():
                copy_x(0, h, x_ref.at[piece(h)], mine, turned).wait_recv()

            @pl.when(jnp.logical_not(moves))
            def _():
                pltpu.make_async_copy(x_ref.at[piece(h)], held.at[mine, piece(h)], x_recv.at[0, h]).wait()

        copy_x(1, h, held.at[mine, piece(h)], mine, across).start()
        copy_x(2, h, held.at[mine, piece(h)], mine, sibling).start()
    for h in range(pieces):
        other = slots[h % 2][1]
        copy_x(1, h, held.at[other, piece(h)], other, across).wait_recv()
        copy_x(3, h, held.at[other, piece(h)], other, sibling).start()
    def block_at(q):
        return lax.rem(ch + q, 2) * subs + lax.rem(sub + q // 2, 2)

    def own(j, h):
        at = pl.ds(pl.multiple_of(j * lanes, lanes), lanes)
        columns = jnp.concatenate([w_ref[g, :, at] for g in range(3)], axis=1)
        acc[...] = jnp.dot(held[h], columns, preferred_element_type=jnp.float32)

    def rising(j, h):
        return pltpu.make_async_remote_copy(
            src_ref=outbox.at[j, h],
            dst_ref=from_below.at[j, h],
            send_sem=box_send.at[j, h],
            recv_sem=below_recv.at[j, h],
            device_id=above,
            device_id_type=MESH,
        )

    def falling(j, h):
        return pltpu.make_async_remote_copy(
            src_ref=outbox.at[j, h],
            dst_ref=from_above.at[j, h],
            send_sem=box_send.at[j, h],
            recv_sem=above_recv.at[j, h],
            device_id=below,
            device_id_type=MESH,
        )

    def add_below(j, h):
        @pl.when(z > 0)
        def _():
            rising(j, h).wait_recv()
            acc[...] += from_below[j, h].astype(jnp.float32)

    def add_above(j, h):
        @pl.when(z < parts - 1)
        def _():
            falling(j, h).wait_recv()
            acc[...] += from_above[j, h].astype(jnp.float32)

    def step(u, _):
        i = u // parts
        h = block_at(lax.rem(u, parts))
        up = parts - 1 - i

        @pl.when(u == 2)
        def _():
            for n in range(pieces):
                copy_x(2 + n % 2, n, held.at[k, piece(n)], k_sibling, sibling).wait_recv()

        @pl.when(u == 3)
        def _():
            for n in range(pieces):
                copy_x(3 - n % 2, n, held.at[k, piece(n)], k_far, sibling).wait_recv()

        @pl.when(up > z)
        def _():
            own(up, h)
            add_below(up, h)
            outbox[up, h] = acc[...].astype(jnp.bfloat16)
            rising(up, h).start()

        @pl.when(i < z)
        def _():
            own(i, h)
            add_above(i, h)
            outbox[i, h] = acc[...].astype(jnp.bfloat16)
            falling(i, h).start()

        return 0

    lax.fori_loop(0, (parts - 1) * parts, step, 0)

    def last(q, _):
        h = block_at(q)
        own(z, h)
        add_below(z, h)
        add_above(z, h)
        for g in range(3):
            out_ref[0, g, pl.ds(pl.multiple_of(h * rows, rows), rows), :] = acc[:, g * lanes : (g + 1) * lanes].astype(jnp.bfloat16)
        return 0

    lax.fori_loop(0, parts, last, 0)

    def drain(u, _):
        j = u // parts
        h = lax.rem(u, parts)

        @pl.when(j != z)
        def _():
            rising(j, h).wait_send()

        return 0

    lax.fori_loop(0, parts * parts, drain, 0)

    @pl.when(moves)
    def _():
        for h in range(0, pieces, 2):
            copy_x(0, h, x_ref.at[piece(h)], z, turned).wait_send()

    for h in range(1, pieces, 2):
        copy_x(0, h, x_ref.at[piece(h)], z, mirrored).wait_send()
    for h in range(pieces):
        for kind in (1, 2, 3):
            copy_x(kind, h, held.at[k, piece(h)], k, sibling).wait_send()


def summed(inputs, weight, parts, subs):
    rows, width = inputs.shape
    lanes = weight.shape[2] // parts
    box = (parts, parts, rows, 3 * lanes)
    dma = pltpu.SemaphoreType.DMA
    return pl.pallas_call(
        functools.partial(partial_sums, parts, subs),
        out_shape=jax.ShapeDtypeStruct((1, 3, rows * parts, lanes), jnp.bfloat16),
        in_specs=[pl.BlockSpec(memory_space=pltpu.VMEM)] * 2,
        out_specs=pl.BlockSpec(memory_space=pltpu.VMEM),
        scratch_shapes=[
            pltpu.VMEM((parts, rows, width), jnp.bfloat16),
            pltpu.VMEM(box, jnp.bfloat16),
            pltpu.VMEM(box, jnp.bfloat16),
            pltpu.VMEM(box, jnp.bfloat16),
            pltpu.VMEM((rows, 3 * lanes), jnp.float32),
            dma((4, 8)),
            dma((4, 8)),
            dma((parts, parts)),
            dma((parts, parts)),
            dma((parts, parts)),
        ],
        compiler_params=pltpu.CompilerParams(
            collective_id=0, has_side_effects=True, vmem_limit_bytes=48 * 2**20
        ),
    )(inputs, weight)


def fast_shards(token_ids, residual_in, embedding, in_weight, short_filter, decay_rate, residue, skip):
    tok_rows, width = residual_in.shape
    vocab_size = embedding.shape[0]
    channels = skip.shape[0]
    seq_parts = lax.axis_size("seq")
    onehot = (token_ids[:, None] == jnp.arange(vocab_size, dtype=jnp.int32)[None, :]).astype(jnp.bfloat16)
    embedded = jnp.dot(onehot, embedding, preferred_element_type=jnp.float32)
    inputs = (residual_in.astype(jnp.float32) + embedded).astype(jnp.bfloat16)
    weight = in_weight.transpose(1, 0, 2)
    partial = summed(inputs, weight, seq_parts, lax.axis_size("sub"))

    mixed = convolved(partial, short_filter, decay_rate, residue, skip)
    return lax.all_to_all(mixed, "seq", split_axis=0, concat_axis=1, tiled=True)


def fits(mesh):
    seq_parts = mesh.shape["seq"]
    return mesh.shape["ch"] == 2 and mesh.shape["sub"] == 2 and seq_parts == mesh.shape["ch"] * mesh.shape["sub"]


def solution(mesh):
    return jax.shard_map(
        fast_shards if fits(mesh) else shards,
        mesh=mesh,
        in_specs=(
            P(("grp", "seq")),
            P(("grp", "seq"), ("ch", "sub")),
            P(None, ("ch", "sub")),
            P("seq", None, ("ch", "sub")),
            P(None, None, ("ch", "sub")),
            P(None, ("ch", "sub")),
            P(None, ("ch", "sub")),
            P(("ch", "sub")),
        ),
        out_specs=P(("grp", "seq"), ("ch", "sub")),
        check_vma=False,
    )
```
